32 devices in a mesh: seg: 4 (over x, core), ops: 8 (over z, y).
Axes of the slice: x: 2, y: 2, z: 4, core: 2. Of those that a mesh axis runs over, the one named last changes fastest.
Arguments:
- amat: bfloat16 [16384, 128], P(('seg', 'ops')), may hold values from -6 to 6
- lam: float32 [16384], P(('seg', 'ops')), may hold values from 0.3 to 3
- hdiag: float32 [16384, 128], P(('seg', 'ops')), may hold values from 0.25 to 8
- left_ops: bfloat16 [4, 48, 4096, 128], P('seg', 'ops'), may hold values from -0.5 to 0.5
- right_operators: bfloat16 [4, 48, 4096, 128], P('seg', 'ops'), may hold values from -0.078125 to 0.078125
- couple: int32 [4, 48, 32], P('seg', 'ops'), may hold values from 0 to 31
- blockmask: int32 [4, 48, 32], P('seg', 'ops'), may hold values 0 or 1
Outputs:
- sigma_two: float32 [16384, 128], P(('seg', 'ops'))
- theta: float32 [4], P('seg')
The draws below stay inside these ranges and needn't reach their ends.
Inputs may be any that keep to these rules, and one draw needn't show every extreme that they name: couple[s, k, i] is the sector of the vector that term k of segment s carries into sector i.
All inputs are finite; a program needn't handle non-finite values. No bound on the sum of `blockmask` on one device may be relied on, other than what follows from the above.
Results may differ from the reference program's by a relative error of at most 0.009.
Values may be sent and summed in bfloat16 or wider, within the bound.
No kernel may reach another device: no remote copies, remote signals or barrier semaphores. Data moves between devices by JAX's collectives and lax.ppermute only.
A program may use at most 64 MiB of HBM per device.

```python
import math
import jax
import jax.numpy as jnp
from jax import lax

M = 4096
NQ = 32
BS = 128
TERMS = 48
SEGS = 4
N_SEG = 4


def draw_hdiag(key, part):
    noise_key = jax.random.fold_in(key, 11)
    row_index = jnp.arange(SEGS * M, dtype=jnp.int32) % M
    segment_position = row_index.astype(jnp.float32) / (M - 1)
    incline = jnp.power(3.0, segment_position)
    texture = jnp.exp(jax.random.uniform(noise_key, (SEGS * M, BS), jnp.float32, -math.log(2.0), math.log(2.0)))
    return (0.5 * incline[:, None] * texture).astype(jnp.float32)


def place_ends(entries, key, smallest, largest):
    place = [jax.random.randint(jax.random.fold_in(key, axis), (), 0, length) for axis, length in enumerate(entries.shape)]
    longest = entries.shape.index(max(entries.shape))
    beside = place[:longest] + [(place[longest] + 1) % entries.shape[longest]] + place[longest + 1:]
    return entries.at[tuple(place)].set(smallest).at[tuple(beside)].set(largest)


def level_of(stream_key, extent, shards, low, largest):
    gain = 1.0
    for axis_at, shards_of in shards:
        draws = jax.random.uniform(jax.random.fold_in(jax.random.fold_in(stream_key, 6), axis_at), (shards_of,), jnp.float32, low / len(shards), largest / len(shards))
        gain = gain * jnp.repeat(jnp.exp(draws), extent[axis_at] // shards_of).reshape((-1,) + (1,) * (len(extent) - 1 - axis_at))
    return gain


def normal_values(rng, dims, spread, reach, shards=(), held_as=jnp.bfloat16):
    result = spread * jax.random.normal(rng, dims, jnp.float32)
    if shards:
        result = result * level_of(rng, dims, shards, -0.22, 0.18)
    return jnp.clip(result, -reach, reach).astype(held_as)


def setup_inputs(seed: int = 0) -> dict:
    key_of = jax.random.split(jax.random.key(seed), 8)
    amat = normal_values(key_of[0], (SEGS * M, BS), 1.0, 6.0, ((0, 32),))
    lam = jnp.clip(jnp.exp(math.log(3.0) - 2.3025851 * jax.random.uniform(key_of[1], (SEGS * M,), jnp.float32) ** level_of(key_of[1], (SEGS * M,), ((0, 32),), -0.2, 0.2)), 0.3, 3.0)
    hdiag = draw_hdiag(jax.random.fold_in(key_of[7], 71), 0)
    left_ops = normal_values(key_of[3], (SEGS, TERMS, M, BS), BS ** -0.5, 0.5, ((0, 4), (1, 8)))
    right_operators = normal_values(key_of[4], (SEGS, TERMS, M, BS), (BS * TERMS) ** -0.5, 0.078125, ((0, 4), (1, 8)))
    couple = place_ends(jax.random.randint(key_of[5], (SEGS, TERMS, NQ), 0, NQ), jax.random.fold_in(key_of[5], 1), 0, NQ - 1).astype(jnp.int32)
    blockmask = place_ends((jax.random.randint(key_of[6], (SEGS, TERMS, NQ), 0, 4) < 3).astype(jnp.int32), jax.random.fold_in(key_of[6], 1), 0, 1)
    return dict(amat=amat, lam=lam, hdiag=hdiag, left_ops=left_ops, right_operators=right_operators, couple=couple, blockmask=blockmask)


def apply_terms(vector, diagonal_entries, left, right, links, live):
    blocks = vector.reshape(NQ, BS, BS).astype(jnp.float32)

    def step(total_sum, index):
        picked = blocks[links[index]]
        lblk = left[index].reshape(NQ, BS, BS).astype(jnp.float32)
        inner_block = jnp.einsum('iab,ibc->iac', lblk, picked)
        inner_block = inner_block * live[index].astype(jnp.float32)[:, None, None]
        inner_block = inner_block.astype(jnp.bfloat16).astype(jnp.float32)
        right_block = right[index].reshape(NQ, BS, BS).astype(jnp.float32)
        return total_sum + jnp.einsum('nwr,nzr->nwz', inner_block, right_block), None

    start = jnp.zeros((NQ, BS, BS), jnp.float32)
    total_sum, unused = lax.scan(step, start, jnp.arange(TERMS, dtype=jnp.int32))
    return total_sum.reshape(M, BS) + diagonal_entries * vector.astype(jnp.float32)


def reference(amat, lam, hdiag, left_ops, right_operators, couple, blockmask):
    output_blocks = []
    quotients = []
    for segment in range(N_SEG):
        lower = segment * M
        upper = lower + M
        tensor = amat[lower:upper].astype(jnp.float32)
        if segment == 0:
            weights = jnp.ones((M,), jnp.float32)
        else:
            weights = lam[lower - M:lower]
        psi = (weights[:, None] * tensor).astype(jnp.bfloat16)
        diagonal_entries = hdiag[lower:upper]
        left = left_ops[segment]
        right = right_operators[segment]
        links = couple[segment]
        live = blockmask[segment]
        sigma_one = apply_terms(psi, diagonal_entries, left, right, links, live)
        psi_float = psi.astype(jnp.float32)
        quotient = jnp.sum(psi_float * sigma_one) / jnp.sum(psi_float * psi_float)
        correction = ((sigma_one - quotient * psi_float) / diagonal_entries).astype(jnp.bfloat16)
        output_blocks.append(apply_terms(correction, diagonal_entries, left, right, links, live))
        quotients.append(quotient)
    return jnp.concatenate(output_blocks, axis=0), jnp.stack(quotients)
```

```python
from functools import partial

import jax
import jax.numpy as jnp
from jax import lax
from jax.experimental import pallas as pl
from jax.experimental.pallas import tpu as pltpu
from jax.sharding import PartitionSpec as P


def shifted(array, axis, by):
    devices = lax.axis_size(axis)
    pairs = [(i, i + by) for i in range(devices) if 0 <= i + by < devices]
    return lax.ppermute(array, axis, pairs)


def row_per_term(blocks, left, right, links, live, width, count):
    nterms = left.shape[0]
    nblock = count // width
    lrows = left.reshape(nterms, nblock, width, width)
    rblock = right.reshape(nterms, nblock, width, width)
    picked = blocks[links]
    inner_block = jnp.einsum("knra,knab->knrb", lrows, picked, preferred_element_type=jnp.float32)
    inner_block = (inner_block * live[:, :, None, None]).astype(jnp.bfloat16)
    result = jnp.einsum("knrb,kndb->nrd", inner_block, rblock, preferred_element_type=jnp.float32)
    return result.reshape(count, width)


def gathered_body(amat, lam, hdiag, left_ops, right_operators, couple, blockmask):
    width = amat.shape[1]
    links = couple[0]
    nsector = links.shape[1]
    bond = width * nsector
    live = blockmask[0].astype(jnp.float32)
    earlier = shifted(lam, "seg", 1)
    weights = jnp.where(lax.axis_index("seg") == 0, jnp.ones_like(earlier), earlier)
    psi = (weights[:, None] * amat.astype(jnp.float32)).astype(jnp.bfloat16)

    def apply_terms(vector):
        whole = lax.all_gather(vector, "ops", axis=0, tiled=True)
        blocks = whole.reshape(nsector, width, width)
        part = row_per_term(blocks, left_ops[0], right_operators[0], links, live, width, bond)
        summed = lax.psum_scatter(part, "ops", scatter_dimension=0, tiled=True)
        return summed + hdiag * vector.astype(jnp.float32)

    sigma_one = apply_terms(psi)
    psi_float = psi.astype(jnp.float32)
    numer, denom = lax.psum((jnp.sum(psi_float * sigma_one), jnp.sum(psi_float * psi_float)), "ops")
    quotient = numer / denom
    correction = ((sigma_one - quotient * psi_float) / hdiag).astype(jnp.bfloat16)
    sigma_two = apply_terms(correction)
    return (sigma_two, quotient.reshape(1))


def terms_kernel(npiece, width, dots, chunk_of, links, left, right, *refs):
    steps = pl.num_programs(0)
    step = pl.program_id(0)
    pieces, refs = refs[:npiece], refs[npiece:]
    vector = refs[-1]
    outs = refs[: len(refs) - 1]
    nterms, rows = left.shape[1], left.shape[2]
    nsector = npiece * rows // width
    per = rows // width

    @pl.when(step == 0)
    def _():
        for p in range(npiece):
            at = pl.multiple_of(chunk_of[steps + p] * rows, rows)
            vector[pl.ds(at, rows), :] = pieces[p][...]
        vector[nsector * width :, :] = jnp.zeros((width, width), vector.dtype)
        if dots:
            outs[-1][...] = jnp.zeros_like(outs[-1])

    chunk = chunk_of[step]
    sums = []
    for i in range(per):
        inner = []
        for k in range(nterms):
            at = pl.multiple_of(links[k * nsector + chunk * per + i] * width, width)
            block = vector[pl.ds(at, width), :]
            lrows = left[0, k, i * width : (i + 1) * width, :]
            inner.append(jnp.dot(lrows, block, preferred_element_type=jnp.float32).astype(jnp.bfloat16))
        rblock = [right[0, k, i * width : (i + 1) * width, :] for k in range(nterms)]
        sums.append(
            lax.dot_general(
                jnp.concatenate(inner, axis=1),
                jnp.concatenate(rblock, axis=1),
                (((1,), (1,)), ((), ())),
                preferred_element_type=jnp.float32,
            )
        )
    total = jnp.concatenate(sums, axis=0)
    nouts = len(outs) - (1 if dots else 0)
    for t in range(nouts):

        @pl.when(step == t)
        def _():
            outs[t][...] = total.astype(outs[t].dtype)

    if dots:
        at = pl.multiple_of(chunk * rows, rows)
        own = vector[pl.ds(at, rows), :].astype(jnp.float32)
        outs[-1][0] += jnp.sum((total * own).reshape(rows // 8, 8, width), axis=0)
        outs[-1][1] += jnp.sum((own * own).reshape(rows // 8, 8, width), axis=0)


def term_rows(left_ops, right_operators, links, chunk_of, steps, pieces, kind, dots):
    _, nterms, bond, width = left_ops.shape
    npiece = len(pieces)
    rows = bond // npiece
    whole = pl.BlockSpec((rows, width), lambda s, *_: (0, 0))
    operator = pl.BlockSpec((1, nterms, rows, width), lambda s, chunk_of, links: (0, 0, chunk_of[s], 0))
    out_shape = [jax.ShapeDtypeStruct((rows, width), kind)] * steps
    out_specs = [whole] * steps
    if dots:
        out_shape.append(jax.ShapeDtypeStruct((2, 8, width), jnp.float32))
        out_specs.append(pl.BlockSpec((2, 8, width), lambda s, *_: (0, 0, 0)))
    flops = 4 * steps * nterms * rows * width * width
    moved = 4 * steps * nterms * rows * width + (npiece + 2 * steps) * rows * width * 2
    return pl.pallas_call(
        partial(terms_kernel, npiece, width, dots),
        grid_spec=pltpu.PrefetchScalarGridSpec(
            num_scalar_prefetch=2,
            grid=(steps,),
            in_specs=[operator, operator] + [whole] * npiece,
            out_specs=out_specs,
            scratch_shapes=[pltpu.VMEM((bond + width, width), jnp.bfloat16)],
        ),
        out_shape=out_shape,
        cost_estimate=pl.CostEstimate(flops=flops, transcendentals=0, bytes_accessed=moved),
        name="term_rows",
    )(chunk_of, links, left_ops, right_operators, *pieces)


def paired_body(amat, lam, hdiag, left_ops, right_operators, couple, blockmask):
    width = amat.shape[1]
    nsector = couple.shape[2]
    devices = lax.axis_size("ops")
    line = devices // 2
    place = lax.axis_index("ops")
    links = jnp.where(blockmask[0] != 0, couple[0], nsector).reshape(-1)

    def along(array, by):
        return lax.ppermute(array, "ops", [(o, o ^ (2 * by)) for o in range(devices)])

    def across(array):
        return lax.ppermute(array, "ops", [(o, o ^ 1) for o in range(devices)])

    near = jnp.stack([place ^ (2 * d) for d in range(line)]).astype(jnp.int32)
    far = near ^ 1
    order = jnp.concatenate([near, far])

    earlier = shifted(lam, "seg", 1)
    weights = jnp.where(lax.axis_index("seg") == 0, jnp.ones_like(earlier), earlier)
    psi = (weights[:, None] * amat.astype(jnp.float32)).astype(jnp.bfloat16)
    psi_float = psi.astype(jnp.float32)

    def gather(piece):
        column = [piece] + [along(piece, d) for d in range(1, line)]
        return column + [across(p) for p in column]

    def apply_terms(piece, dots):
        pieces = gather(piece)
        sent = term_rows(left_ops, right_operators, links, jnp.concatenate([far, order]), line, pieces, jnp.bfloat16, dots)
        kept = term_rows(left_ops, right_operators, links, jnp.concatenate([near, order]), line, pieces, jnp.float32, dots)
        came = [across(s) for s in sent[:line]]
        both = [k + c.astype(jnp.float32) for k, c in zip(kept[:line], came)]
        total = both[0]
        for d in range(1, line):
            total = total + along(both[d].astype(jnp.bfloat16), d).astype(jnp.float32)
        return total + hdiag * piece.astype(jnp.float32), (sent[line] + kept[line]) if dots else None

    sigma_one, sums = apply_terms(psi, True)
    diagonal = jnp.sum((hdiag * psi_float * psi_float).reshape(-1, 8, width), axis=0)
    numer = sums[0] + diagonal
    numer = numer + across(numer)
    step = 1
    while step < line:
        numer = numer + along(numer, step)
        step *= 2
    quotient = jnp.sum(numer) / jnp.sum(sums[1])
    correction = ((sigma_one - quotient * psi_float) / hdiag).astype(jnp.bfloat16)
    sigma_two, _ = apply_terms(correction, False)
    return (sigma_two, quotient.reshape(1))


def body(amat, lam, hdiag, left_ops, right_operators, couple, blockmask):
    devices = lax.axis_size("ops")
    paired = devices >= 2 and devices & (devices - 1) == 0 and couple.shape[2] % devices == 0
    form = paired_body if paired else gathered_body
    return form(amat, lam, hdiag, left_ops, right_operators, couple, blockmask)


def solution(mesh):
    placed = (
        P(("seg", "ops"), None),
        P(("seg", "ops")),
        P(("seg", "ops"), None),
        P("seg", "ops", None, None),
        P("seg", "ops", None, None),
        P("seg", "ops", None),
        P("seg", "ops", None),
    )
    return jax.shard_map(
        body,
        mesh=mesh,
        in_specs=placed,
        out_specs=(P(("seg", "ops"), None), P("seg")),
        check_vma=False,
    )
```

```python
from functools import partial

import jax
import jax.numpy as jnp
from jax import lax
from jax.experimental import pallas as pl
from jax.experimental.pallas import tpu as pltpu
from jax.sharding import PartitionSpec as P


def shifted(array, axis, by):
    devices = lax.axis_size(axis)
    pairs = [(i, i + by) for i in range(devices) if 0 <= i + by < devices]
    return lax.ppermute(array, axis, pairs)


def row_per_term(blocks, left, right, links, live, width, count):
    nterms = left.shape[0]
    nblock = count // width
    lrows = left.reshape(nterms, nblock, width, width)
    rblock = right.reshape(nterms, nblock, width, width)
    picked = blocks[links]
    inner_block = jnp.einsum("knra,knab->knrb", lrows, picked, preferred_element_type=jnp.float32)
    inner_block = (inner_block * live[:, :, None, None]).astype(jnp.bfloat16)
    result = jnp.einsum("knrb,kndb->nrd", inner_block, rblock, preferred_element_type=jnp.float32)
    return result.reshape(count, width)


def gathered_body(amat, lam, hdiag, left_ops, right_operators, couple, blockmask):
    width = amat.shape[1]
    links = couple[0]
    nsector = links.shape[1]
    bond = width * nsector
    live = blockmask[0].astype(jnp.float32)
    earlier = shifted(lam, "seg", 1)
    weights = jnp.where(lax.axis_index("seg") == 0, jnp.ones_like(earlier), earlier)
    psi = (weights[:, None] * amat.astype(jnp.float32)).astype(jnp.bfloat16)

    def apply_terms(vector):
        whole = lax.all_gather(vector, "ops", axis=0, tiled=True)
        blocks = whole.reshape(nsector, width, width)
        part = row_per_term(blocks, left_ops[0], right_operators[0], links, live, width, bond)
        summed = lax.psum_scatter(part, "ops", scatter_dimension=0, tiled=True)
        return summed + hdiag * vector.astype(jnp.float32)

    sigma_one = apply_terms(psi)
    psi_float = psi.astype(jnp.float32)
    numer, denom = lax.psum((jnp.sum(psi_float * sigma_one), jnp.sum(psi_float * psi_float)), "ops")
    quotient = numer / denom
    correction = ((sigma_one - quotient * psi_float) / hdiag).astype(jnp.bfloat16)
    sigma_two = apply_terms(correction)
    return (sigma_two, quotient.reshape(1))


def scaled_products(vector, links, left, right, chunks, per, store):
    nterms, width = left.shape[1], left.shape[3]
    nsector = vector.shape[0] // width - 1

    def inner_of(i):
        rows = pl.ds(pl.multiple_of(i * width, width), width)
        blocks = []
        for k in range(nterms):
            at = pl.multiple_of(links[k * nsector + i] * width, width)
            product = jnp.dot(left[0, k, rows, :], vector[pl.ds(at, width), :], preferred_element_type=jnp.float32)
            blocks.append(product.astype(jnp.bfloat16))
        return jnp.concatenate(blocks, axis=1), rows

    def outer_of(inner, rows):
        factors = jnp.concatenate([right[0, k, rows, :] for k in range(nterms)], axis=1)
        return lax.dot_general(inner, factors, (((1,), (1,)), ((), ())), preferred_element_type=jnp.float32)

    waiting = None
    for t, chunk in enumerate(chunks):
        for i in range(per):
            now = inner_of(chunk * per + i)
            if waiting is not None:
                store(*waiting[:2], outer_of(*waiting[2]))
            waiting = (t, i, now)
    store(*waiting[:2], outer_of(*waiting[2]))


def rows_at(chunk, rows):
    return pl.ds(pl.multiple_of(chunk * rows, rows), rows)


def squares(total, own):
    return jnp.sum((total * own).reshape(-1, 8, total.shape[1]), axis=0)


def first_kernel(line, first, dots, place, links, left, right, *refs):
    npiece = 2 * line
    pieces, vector, outs = refs[:npiece], refs[npiece], refs[npiece + 1 :]
    rows, width = pieces[0].shape
    for p in range(npiece):
        chunk = place[0] ^ (2 * (p % line)) ^ (p // line)
        vector[rows_at(chunk, rows), :] = pieces[p][...]
    vector[npiece * rows :, :] = jnp.zeros((width, width), vector.dtype)
    chunks = [place[0] ^ (2 * d) ^ 1 for d in first]
    if dots:
        outs[-1][...] = jnp.zeros_like(outs[-1])

    def store(t, i, sums):
        at = slice(i * width, (i + 1) * width)
        outs[t][at, :] = sums.astype(outs[t].dtype)
        if dots:
            start = pl.multiple_of(chunks[t] * rows + i * width, width)
            outs[-1][...] += squares(sums, vector[pl.ds(start, width), :].astype(jnp.float32))

    scaled_products(vector, links, left, right, chunks, rows // width, store)


def second_kernel(line, rest, dots, place, links, left, right, vector, *refs):
    width = vector.shape[1]
    if dots:
        hdiag, before, *outs, numer, denom = refs
        rows = hdiag.shape[0]
        own = vector[rows_at(place[0], rows), :].astype(jnp.float32)
        numer[...] = before[...] + squares(hdiag[...] * own, own)
        whole = vector[: 2 * line * rows, :].astype(jnp.float32)
        denom[...] = squares(whole, whole)
    else:
        outs = refs
        rows = outs[0].shape[0]
    chunks = [place[0] ^ (2 * d) ^ 1 for d in rest] + [place[0] ^ (2 * d) for d in range(line)]

    def store(t, i, sums):
        at = slice(i * width, (i + 1) * width)
        outs[t][at, :] = sums.astype(outs[t].dtype)
        if dots:
            start = pl.multiple_of(chunks[t] * rows + i * width, width)
            numer[...] += squares(sums, vector[pl.ds(start, width), :].astype(jnp.float32))

    scaled_products(vector, links, left, right, chunks, rows // width, store)


TAIL = 16


def pass_kernel(kept, came, mine, other, out):
    rows, width = kept.shape
    out[:rows, :] = (kept[...] + came[...].astype(jnp.float32)).astype(out.dtype)
    part = jnp.sum(mine[...] + other[...], axis=0, keepdims=True)
    row = lax.broadcasted_iota(jnp.int32, (TAIL, width), 0)
    tail = jnp.zeros((TAIL, width), jnp.float32)
    for r in range(3):
        rounded = part.astype(out.dtype).astype(jnp.float32)
        tail = jnp.where(row == r, rounded, tail)
        part = part - rounded
    out[rows:, :] = tail.astype(out.dtype)


def correct_kernel(nmore, *refs):
    kept, came, more, refs = refs[0], refs[1], refs[2 : 2 + nmore], refs[2 + nmore :]
    psi, hdiag, mine, other, denom, correction, theta = refs
    rows = psi.shape[0]
    total = kept[...] + came[...].astype(jnp.float32)
    numer = jnp.sum(mine[...] + other[...], keepdims=True)
    for m in more:
        total = total + m[:rows, :].astype(jnp.float32)
        numer = numer + jnp.sum(m[rows:, :].astype(jnp.float32), keepdims=True)
    quotient = numer / jnp.sum(denom[...], keepdims=True)
    vector = psi[...].astype(jnp.float32)
    sigma = total + hdiag[...] * vector
    correction[...] = ((sigma - quotient * vector) / hdiag[...]).astype(correction.dtype)
    theta[...] = jnp.broadcast_to(quotient, theta.shape)


def load_kernel(source, target, sems):
    copies = [pltpu.make_async_copy(source.at[:, k], target.at[:, k], sems.at[k]) for k in range(source.shape[1])]
    for copy in copies:
        copy.start()
    for copy in copies:
        copy.wait()


VMEM = pl.BlockSpec(memory_space=pltpu.VMEM)
SMEM = pl.BlockSpec(memory_space=pltpu.SMEM)


def on_chip(kernel, out_shape, nscalar, *args, limit=8 << 20):
    outs = pl.pallas_call(
        kernel,
        out_shape=out_shape,
        in_specs=[SMEM] * nscalar + [VMEM] * (len(args) - nscalar),
        out_specs=[VMEM] * len(out_shape),
        compiler_params=pltpu.CompilerParams(vmem_limit_bytes=limit),
    )(*args)
    return list(outs)


def loaded(operators):
    return pl.pallas_call(
        load_kernel,
        out_shape=pltpu.VMEM(operators.shape, operators.dtype),
        in_specs=[pl.BlockSpec(memory_space=pltpu.HBM)],
        out_specs=VMEM,
        scratch_shapes=[pltpu.SemaphoreType.DMA((operators.shape[1],))],
        compiler_params=pltpu.CompilerParams(vmem_limit_bytes=1 << 20),
    )(pltpu.with_memory_space_constraint(operators, pltpu.HBM))


def far_first(line):
    return sorted(range(line), key=lambda d: -d.bit_length())


def paired_body(amat, lam, hdiag, left_ops, right_operators, couple, blockmask):
    rows, width = amat.shape
    nsector = couple.shape[2]
    devices = lax.axis_size("ops")
    line = devices // 2
    place = lax.axis_index("ops").astype(jnp.int32).reshape(1)
    links = jnp.where(blockmask[0] != 0, couple[0], nsector).reshape(-1)
    shape = jax.ShapeDtypeStruct
    tile = shape((8, width), jnp.float32)
    sent, kept = shape((rows, width), jnp.bfloat16), shape((rows, width), jnp.float32)

    def exchange(array, by):
        return lax.ppermute(array, "ops", [(o, o ^ by) for o in range(devices)])

    far = far_first(line)
    first, rest = far[:1], far[1:]

    def gather(piece):
        column = {0: piece}
        for d in far:
            if d:
                column[d] = exchange(piece, 2 * d)
        other = {d: exchange(column[d], 1) for d in range(line)}
        return [column[d] for d in range(line)] + [other[d] for d in range(line)]

    def apply_terms(piece, left, right, dots):
        left = pltpu.with_memory_space_constraint(left, pltpu.VMEM)
        right = pltpu.with_memory_space_constraint(right, pltpu.VMEM)
        pieces = gather(piece)
        whole = shape((devices * rows + width, width), jnp.bfloat16)
        vector, *lead = on_chip(
            partial(first_kernel, line, first, dots),
            [whole] + [sent] * len(first) + [tile] * dots,
            2, place, links, left, right, *pieces,
        )
        extra = (hdiag, lead[-1]) if dots else ()
        outs = on_chip(
            partial(second_kernel, line, rest, dots),
            [sent] * len(rest) + [kept] * line + [tile] * (2 * dots),
            2, place, links, left, right, vector, *extra,
        )
        leave = dict(zip(first + rest, lead[: len(first)] + outs[: len(rest)]))
        stay = outs[len(rest) : len(rest) + line]
        sums = ()
        if dots:
            mine, denom = outs[len(rest) + line :]
            other = exchange(mine, 1)
            sums = (mine, other, denom)
        came = {d: exchange(leave[d], 1) for d in far}
        more = []
        for d in far:
            if d and dots:
                message = on_chip(pass_kernel, [shape((rows + TAIL, width), jnp.bfloat16)], 0, stay[d], came[d], mine, other)[0]
            elif d:
                message = (stay[d] + came[d].astype(jnp.float32)).astype(jnp.bfloat16)
            if d:
                more.append(exchange(message, 2 * d))
        return [stay[0], came[0]] + more, sums

    links, left_ops, right_operators = lax.optimization_barrier((links, left_ops, right_operators))
    left = loaded(left_ops)
    right = loaded(right_operators)
    earlier = shifted(lam, "seg", 1)
    weights = jnp.where(lax.axis_index("seg") == 0, jnp.ones_like(earlier), earlier)
    psi = (weights[:, None] * amat.astype(jnp.float32)).astype(jnp.bfloat16)
    terms, sums = apply_terms(psi, left, right, True)
    correction, theta = on_chip(partial(correct_kernel, line - 1), [sent, tile], 0, *terms, psi, hdiag, *sums)
    terms, _ = apply_terms(correction, left, right, False)
    sigma_two = sum(t.astype(jnp.float32) for t in terms) + hdiag * correction.astype(jnp.float32)
    return (sigma_two, theta[0, :1])


def is_paired(devices, nsector):
    return devices >= 2 and devices & (devices - 1) == 0 and nsector % devices == 0


def body(amat, lam, hdiag, left_ops, right_operators, couple, blockmask):
    form = paired_body if is_paired(lax.axis_size("ops"), couple.shape[2]) else gathered_body
    return form(amat, lam, hdiag, left_ops, right_operators, couple, blockmask)


def solution(mesh):
    placed = (
        P(("seg", "ops"), None),
        P(("seg", "ops")),
        P(("seg", "ops"), None),
        P("seg", "ops", None, None),
        P("seg", "ops", None, None),
        P("seg", "ops", None),
        P("seg", "ops", None),
    )
    return jax.shard_map(
        body,
        mesh=mesh,
        in_specs=placed,
        out_specs=(P(("seg", "ops"), None), P("seg")),
        check_vma=False,
    )
```

```python
from functools import partial

import jax
import jax.numpy as jnp
from jax import lax
from jax.experimental import pallas as pl
from jax.experimental.pallas import tpu as pltpu
from jax.sharding import PartitionSpec as P


def shifted(array, axis, by):
    devices = lax.axis_size(axis)
    pairs = [(i, i + by) for i in range(devices) if 0 <= i + by < devices]
    return lax.ppermute(array, axis, pairs)


def row_per_term(blocks, left, right, links, live, width, count):
    nterms = left.shape[0]
    nblock = count // width
    lrows = left.reshape(nterms, nblock, width, width)
    rblock = right.reshape(nterms, nblock, width, width)
    picked = blocks[links]
    inner_block = jnp.einsum("knra,knab->knrb", lrows, picked, preferred_element_type=jnp.float32)
    inner_block = (inner_block * live[:, :, None, None]).astype(jnp.bfloat16)
    result = jnp.einsum("knrb,kndb->nrd", inner_block, rblock, preferred_element_type=jnp.float32)
    return result.reshape(count, width)


def gathered_body(amat, lam, hdiag, left_ops, right_operators, couple, blockmask):
    width = amat.shape[1]
    links = couple[0]
    nsector = links.shape[1]
    bond = width * nsector
    live = blockmask[0].astype(jnp.float32)
    earlier = shifted(lam, "seg", 1)
    weights = jnp.where(lax.axis_index("seg") == 0, jnp.ones_like(earlier), earlier)
    psi = (weights[:, None] * amat.astype(jnp.float32)).astype(jnp.bfloat16)

    def apply_terms(vector):
        whole = lax.all_gather(vector, "ops", axis=0, tiled=True)
        blocks = whole.reshape(nsector, width, width)
        part = row_per_term(blocks, left_ops[0], right_operators[0], links, live, width, bond)
        summed = lax.psum_scatter(part, "ops", scatter_dimension=0, tiled=True)
        return summed + hdiag * vector.astype(jnp.float32)

    sigma_one = apply_terms(psi)
    psi_float = psi.astype(jnp.float32)
    numer, denom = lax.psum((jnp.sum(psi_float * sigma_one), jnp.sum(psi_float * psi_float)), "ops")
    quotient = numer / denom
    correction = ((sigma_one - quotient * psi_float) / hdiag).astype(jnp.bfloat16)
    sigma_two = apply_terms(correction)
    return (sigma_two, quotient.reshape(1))


def scaled_products(vector, links, left, right, chunks, per, store):
    nterms, width = left.shape[1], left.shape[3]
    nsector = vector.shape[0] // width - 1

    def inner_of(i):
        rows = pl.ds(pl.multiple_of(i * width, width), width)
        blocks = []
        for k in range(nterms):
            at = pl.multiple_of(links[k * nsector + i] * width, width)
            product = jnp.dot(left[0, k, rows, :], vector[pl.ds(at, width), :], preferred_element_type=jnp.float32)
            blocks.append(product.astype(jnp.bfloat16))
        return jnp.concatenate(blocks, axis=1), rows

    def outer_of(inner, rows):
        factors = jnp.concatenate([right[0, k, rows, :] for k in range(nterms)], axis=1)
        return lax.dot_general(inner, factors, (((1,), (1,)), ((), ())), preferred_element_type=jnp.float32)

    waiting = None
    for t, chunk in enumerate(chunks):
        for i in range(per):
            now = inner_of(chunk * per + i)
            if waiting is not None:
                store(*waiting[:2], outer_of(*waiting[2]))
            waiting = (t, i, now)
    store(*waiting[:2], outer_of(*waiting[2]))


def rows_at(chunk, rows):
    return pl.ds(pl.multiple_of(chunk * rows, rows), rows)


def squares(total, own):
    return jnp.sum((total * own).reshape(-1, 8, total.shape[1]), axis=0)


TAIL = 16


def first_kernel(offsets, first, dots, place, links, left, right, *refs):
    npiece = len(offsets)
    pieces, vector, outs = refs[:npiece], refs[npiece], refs[npiece + 1 :]
    rows, width = pieces[0].shape
    for piece, offset in zip(pieces, offsets):
        vector[rows_at(place[0] ^ offset, rows), :] = piece[...]
    vector[npiece * rows :, :] = jnp.zeros((width, width), vector.dtype)
    chunks = [place[0] ^ offset for offset in first]
    if dots:
        outs[-1][...] = jnp.zeros_like(outs[-1])

    def store(t, i, sums):
        at = slice(i * width, (i + 1) * width)
        outs[t][at, :] = sums.astype(outs[t].dtype)
        if dots:
            start = pl.multiple_of(chunks[t] * rows + i * width, width)
            outs[-1][...] += squares(sums, vector[pl.ds(start, width), :].astype(jnp.float32))

    scaled_products(vector, links, left, right, chunks, rows // width, store)


def three_roundings(part):
    row = lax.broadcasted_iota(jnp.int32, (TAIL, part.shape[1]), 0)
    tail = jnp.zeros((TAIL, part.shape[1]), jnp.float32)
    for r in range(3):
        rounded = part.astype(jnp.bfloat16).astype(jnp.float32)
        tail = jnp.where(row == r, rounded, tail)
        part = part - rounded
    return tail.astype(jnp.bfloat16)


def second_kernel(rest, dots, place, links, left, right, vector, *refs):
    width = vector.shape[1]
    if dots:
        hdiag, before, *outs, numer, denom = refs
        rows = hdiag.shape[0]
        own = vector[rows_at(place[0], rows), :].astype(jnp.float32)
        numer[...] = before[...] + squares(hdiag[...] * own, own)
        whole = vector[: vector.shape[0] - width, :].astype(jnp.float32)
        denom[...] = squares(whole, whole)
    else:
        outs = refs
        rows = outs[0].shape[0]
    chunks = [place[0] ^ offset for offset in rest]

    def store(t, i, sums):
        at = slice(i * width, (i + 1) * width)
        outs[t][at, :] = sums.astype(outs[t].dtype)
        if dots:
            start = pl.multiple_of(chunks[t] * rows + i * width, width)
            numer[...] += squares(sums, vector[pl.ds(start, width), :].astype(jnp.float32))

    scaled_products(vector, links, left, right, chunks, rows // width, store)
    if dots:
        tail = three_roundings(jnp.sum(numer[...], axis=0, keepdims=True))
        for out in outs:
            if out.shape[0] > rows:
                out[rows:, :] = tail


def added_kernel(kept, *refs):
    out = refs[-1]
    total = kept[...]
    for came in refs[:-1]:
        total = total + came[...].astype(jnp.float32)
    out[...] = total.astype(out.dtype)


def half_kernel(numer, *refs):
    out = refs[-1]
    total = jnp.sum(numer[...], axis=0, keepdims=True)
    for came in refs[:-1]:
        rows = came.shape[0] - TAIL
        total = total + jnp.sum(came[rows:, :].astype(jnp.float32), axis=0, keepdims=True)
    out[...] = jnp.broadcast_to(total, out.shape)


def correct_kernel(nmore, *refs):
    kept, more, refs = refs[0], refs[1 : 1 + nmore], refs[1 + nmore :]
    psi, hdiag, mine, other, denom, correction, theta = refs
    rows = psi.shape[0]
    total = kept[...]
    for m in more:
        total = total + m[:rows, :].astype(jnp.float32)
    numer = jnp.sum(mine[:1, :] + other[:1, :], keepdims=True)
    quotient = numer / jnp.sum(denom[...], keepdims=True)
    vector = psi[...].astype(jnp.float32)
    sigma = total + hdiag[...] * vector
    correction[...] = ((sigma - quotient * vector) / hdiag[...]).astype(correction.dtype)
    theta[...] = jnp.broadcast_to(quotient, theta.shape)


def load_kernel(source, target, sems):
    copies = [pltpu.make_async_copy(source.at[:, k], target.at[:, k], sems.at[k]) for k in range(source.shape[1])]
    for copy in copies:
        copy.start()
    for copy in copies:
        copy.wait()


VMEM = pl.BlockSpec(memory_space=pltpu.VMEM)
SMEM = pl.BlockSpec(memory_space=pltpu.SMEM)


def on_chip(kernel, out_shape, nscalar, *args, limit=8 << 20):
    outs = pl.pallas_call(
        kernel,
        out_shape=out_shape,
        in_specs=[SMEM] * nscalar + [VMEM] * (len(args) - nscalar),
        out_specs=[VMEM] * len(out_shape),
        compiler_params=pltpu.CompilerParams(vmem_limit_bytes=limit),
    )(*args)
    return list(outs)


def loaded(operators):
    return pl.pallas_call(
        load_kernel,
        out_shape=pltpu.VMEM(operators.shape, operators.dtype),
        in_specs=[pl.BlockSpec(memory_space=pltpu.HBM)],
        out_specs=VMEM,
        scratch_shapes=[pltpu.SemaphoreType.DMA((operators.shape[1],))],
        compiler_params=pltpu.CompilerParams(vmem_limit_bytes=1 << 20),
    )(pltpu.with_memory_space_constraint(operators, pltpu.HBM))


def within(half):
    return sorted(range(1, half), key=lambda r: (-r.bit_count(), r))


def paired_body(amat, lam, hdiag, left_ops, right_operators, couple, blockmask):
    rows, width = amat.shape
    nsector = couple.shape[2]
    devices = lax.axis_size("ops")
    half = devices // 2
    inside = within(half)
    place = lax.axis_index("ops").astype(jnp.int32).reshape(1)
    links = jnp.where(blockmask[0] != 0, couple[0], nsector).reshape(-1)
    shape = jax.ShapeDtypeStruct
    tile = shape((8, width), jnp.float32)
    sent, kept = shape((rows, width), jnp.bfloat16), shape((rows, width), jnp.float32)
    tailed = shape((rows + TAIL, width), jnp.bfloat16)

    def exchange(array, by):
        return lax.ppermute(array, "ops", [(o, o ^ by) for o in range(devices)])

    def gather(piece):
        pieces = {0: piece, half: exchange(piece, half)}
        for r in inside:
            pieces[r] = exchange(piece, r)
        for r in inside:
            pieces[half ^ r] = exchange(pieces[half], r)
        return pieces

    def apply_terms(piece, left, right, dots):
        left = pltpu.with_memory_space_constraint(left, pltpu.VMEM)
        right = pltpu.with_memory_space_constraint(right, pltpu.VMEM)
        pieces = gather(piece)
        first = [half ^ r for r in inside]
        rest = inside + [half, 0]
        whole = shape((devices * rows + width, width), jnp.bfloat16)
        vector, *lead = on_chip(
            partial(first_kernel, list(pieces), first, dots),
            [whole] + [sent] * len(first) + [tile] * dots,
            2, place, links, left, right, *pieces.values(),
        )
        extra = (hdiag, lead[-1]) if dots else ()
        outs = on_chip(
            partial(second_kernel, rest, dots),
            [tailed if dots else sent] * len(inside) + [kept] * 2 + [tile] * (2 * dots),
            2, place, links, left, right, vector, *extra,
        )
        crossing, own, *sums = outs[len(inside) :]
        came = [exchange(chunk, r) for r, chunk in zip(inside, lead)]
        ours = [exchange(chunk, r) for r, chunk in zip(inside, outs)]
        theirs = exchange(on_chip(added_kernel, [sent], 0, crossing, *came)[0], half)
        if dots:
            numer, denom = sums
            mine = on_chip(half_kernel, [tile], 0, numer, *ours)[0]
            sums = [mine, exchange(mine, half), denom]
        return [own, *ours, theirs], sums

    place, links, left_ops, right_operators = lax.optimization_barrier((place, links, left_ops, right_operators))
    left = loaded(left_ops)
    right = loaded(right_operators)
    earlier = shifted(lam, "seg", 1)
    weights = jnp.where(lax.axis_index("seg") == 0, jnp.ones_like(earlier), earlier)
    psi = (weights[:, None] * amat.astype(jnp.float32)).astype(jnp.bfloat16)
    terms, sums = apply_terms(psi, left, right, True)
    correction, theta = on_chip(partial(correct_kernel, half), [sent, tile], 0, *terms, psi, hdiag, *sums)
    terms, _ = apply_terms(correction, left, right, False)
    sigma_two = sum(t.astype(jnp.float32) for t in terms) + hdiag * correction.astype(jnp.float32)
    return (sigma_two, theta[0, :1])


def is_paired(devices, nsector):
    return devices >= 4 and devices & (devices - 1) == 0 and nsector % devices == 0


def body(amat, lam, hdiag, left_ops, right_operators, couple, blockmask):
    form = paired_body if is_paired(lax.axis_size("ops"), couple.shape[2]) else gathered_body
    return form(amat, lam, hdiag, left_ops, right_operators, couple, blockmask)


def solution(mesh):
    placed = (
        P(("seg", "ops"), None),
        P(("seg", "ops")),
        P(("seg", "ops"), None),
        P("seg", "ops", None, None),
        P("seg", "ops", None, None),
        P("seg", "ops", None),
        P("seg", "ops", None),
    )
    return jax.shard_map(
        body,
        mesh=mesh,
        in_specs=placed,
        out_specs=(P(("seg", "ops"), None), P("seg")),
        check_vma=False,
    )
```

```python
from functools import partial

import jax
import jax.numpy as jnp
from jax import lax
from jax.experimental import pallas as pl
from jax.experimental.pallas import tpu as pltpu
from jax.sharding import PartitionSpec as P


def shifted(array, axis, by):
    devices = lax.axis_size(axis)
    pairs = [(i, i + by) for i in range(devices) if 0 <= i + by < devices]
    return lax.ppermute(array, axis, pairs)


def row_per_term(blocks, left, right, links, live, width, count):
    nterms = left.shape[0]
    nblock = count // width
    lrows = left.reshape(nterms, nblock, width, width)
    rblock = right.reshape(nterms, nblock, width, width)
    picked = blocks[links]
    inner_block = jnp.einsum("knra,knab->knrb", lrows, picked, preferred_element_type=jnp.float32)
    inner_block = (inner_block * live[:, :, None, None]).astype(jnp.bfloat16)
    result = jnp.einsum("knrb,kndb->nrd", inner_block, rblock, preferred_element_type=jnp.float32)
    return result.reshape(count, width)


def gathered_body(amat, lam, hdiag, left_ops, right_operators, couple, blockmask):
    width = amat.shape[1]
    links = couple[0]
    nsector = links.shape[1]
    bond = width * nsector
    live = blockmask[0].astype(jnp.float32)
    earlier = shifted(lam, "seg", 1)
    weights = jnp.where(lax.axis_index("seg") == 0, jnp.ones_like(earlier), earlier)
    psi = (weights[:, None] * amat.astype(jnp.float32)).astype(jnp.bfloat16)

    def apply_terms(vector):
        whole = lax.all_gather(vector, "ops", axis=0, tiled=True)
        blocks = whole.reshape(nsector, width, width)
        part = row_per_term(blocks, left_ops[0], right_operators[0], links, live, width, bond)
        summed = lax.psum_scatter(part, "ops", scatter_dimension=0, tiled=True)
        return summed + hdiag * vector.astype(jnp.float32)

    sigma_one = apply_terms(psi)
    psi_float = psi.astype(jnp.float32)
    numer, denom = lax.psum((jnp.sum(psi_float * sigma_one), jnp.sum(psi_float * psi_float)), "ops")
    quotient = numer / denom
    correction = ((sigma_one - quotient * psi_float) / hdiag).astype(jnp.bfloat16)
    sigma_two = apply_terms(correction)
    return (sigma_two, quotient.reshape(1))


def scaled_products(vector, links, left, right, chunks, per, store):
    width = vector.shape[1]
    nsector = vector.shape[0] // width - 1
    nterms = left.shape[0]

    def inner_of(i):
        rows = pl.ds(pl.multiple_of(i * width, width), width)
        blocks = []
        for k in range(nterms):
            at = pl.multiple_of(links[k * nsector + i] * width, width)
            product = jnp.dot(left[k, rows, :], vector[pl.ds(at, width), :], preferred_element_type=jnp.float32)
            blocks.append(product.astype(jnp.bfloat16))
        return jnp.concatenate(blocks, axis=1), rows

    def outer_of(inner, rows):
        factors = jnp.concatenate([right[k, rows, :] for k in range(nterms)], axis=1)
        return lax.dot_general(inner, factors, (((1,), (1,)), ((), ())), preferred_element_type=jnp.float32)

    waiting = None
    for t, chunk in enumerate(chunks):
        for i in range(per):
            now = inner_of(chunk * per + i)
            if waiting is not None:
                store(*waiting[:2], outer_of(*waiting[2]))
            waiting = (t, i, now)
    store(*waiting[:2], outer_of(*waiting[2]))


def rows_at(chunk, rows):
    return pl.ds(pl.multiple_of(chunk * rows, rows), rows)


def squares(total, own):
    return jnp.sum((total * own).reshape(-1, 8, total.shape[1]), axis=0)


TAIL = 16


def chunk_sums(offsets, rows, place, links, left, right, vector, outs, numer):
    width = vector.shape[1]
    chunks = [place[0] ^ offset for offset in offsets]

    def store(t, i, sums):
        at = slice(i * width, (i + 1) * width)
        outs[t][at, :] = sums.astype(outs[t].dtype)
        if numer is not None:
            start = pl.multiple_of(chunks[t] * rows + i * width, width)
            numer[...] += squares(sums, vector[pl.ds(start, width), :].astype(jnp.float32))

    scaled_products(vector, links, left, right, chunks, rows // width, store)


def first_kernel(offsets, first, dots, place, links, left, right, *refs):
    npiece = len(offsets)
    pieces, vector, outs = refs[:npiece], refs[npiece], refs[npiece + 1 :]
    rows, width = pieces[0].shape
    for piece, offset in zip(pieces, offsets):
        vector[rows_at(place[0] ^ offset, rows), :] = piece[...]
    vector[npiece * rows :, :] = jnp.zeros((width, width), vector.dtype)
    numer = outs[-1] if dots else None
    if dots:
        numer[...] = jnp.zeros_like(numer)
    chunk_sums(first, rows, place, links, left, right, vector, outs, numer)


def last_kernel(offsets, dots, place, links, left, right, vector, *refs):
    width = vector.shape[1]
    numer = None
    rows = refs[-1].shape[0]
    if dots:
        hdiag, before, *refs, numer, denom = refs
        rows = hdiag.shape[0]
        own = vector[rows_at(place[0], rows), :].astype(jnp.float32)
        numer[...] = before[...] + squares(hdiag[...] * own, own)
        whole = vector[: vector.shape[0] - width, :].astype(jnp.float32)
        denom[...] = squares(whole, whole)
    chunk_sums(offsets, rows, place, links, left, right, vector, refs, numer)


def three_roundings(part):
    row = lax.broadcasted_iota(jnp.int32, (TAIL, part.shape[1]), 0)
    tail = jnp.zeros((TAIL, part.shape[1]), jnp.float32)
    for r in range(3):
        rounded = part.astype(jnp.bfloat16).astype(jnp.float32)
        tail = jnp.where(row == r, rounded, tail)
        part = part - rounded
    return tail.astype(jnp.bfloat16)


def tail_kernel(nlate, mine, other, *refs):
    chunks, both, outs = refs[:nlate], refs[nlate], refs[nlate + 1 :]
    both[...] = mine[...] + other[...]
    tail = three_roundings(jnp.sum(both[...], axis=0, keepdims=True))
    for chunk, out in zip(chunks, outs):
        rows = chunk.shape[0]
        out[:rows, :] = chunk[...]
        out[rows:, :] = tail


def added_kernel(kept, *refs):
    out = refs[-1]
    total = kept[...]
    for came in refs[:-1]:
        total = total + came[...].astype(jnp.float32)
    out[...] = total.astype(out.dtype)


def final_kernel(kept, vector, hdiag, *refs):
    out = refs[-1]
    total = kept[...] + hdiag[...] * vector[...].astype(jnp.float32)
    for came in refs[:-1]:
        total = total + came[...].astype(jnp.float32)
    out[...] = total


def correct_kernel(nmore, *refs):
    kept, more, refs = refs[0], refs[1 : 1 + nmore], refs[1 + nmore :]
    psi, hdiag, mine, other, denom, correction, theta = refs
    rows = psi.shape[0]
    total = kept[...]
    numer = jnp.sum(mine[...] + other[...], keepdims=True)
    for m in more:
        total = total + m[:rows, :].astype(jnp.float32)
        if m.shape[0] > rows:
            numer = numer + jnp.sum(m[rows:, :].astype(jnp.float32), keepdims=True)
    quotient = numer / jnp.sum(denom[...], keepdims=True)
    vector = psi[...].astype(jnp.float32)
    sigma = total + hdiag[...] * vector
    correction[...] = ((sigma - quotient * vector) / hdiag[...]).astype(correction.dtype)
    theta[...] = jnp.broadcast_to(quotient, theta.shape)


def weigh_kernel(weights, piece, out):
    width = out.shape[1]
    columns = weights[...].T
    for i in range(weights.shape[0]):
        at = slice(i * width, (i + 1) * width)
        out[at, :] = (columns[:, i : i + 1] * piece[at, :].astype(jnp.float32)).astype(out.dtype)


def load_kernel(source, target, sems):
    count = sems.shape[0]
    step = source.shape[0] // count
    copies = [pltpu.make_async_copy(source.at[at], target.at[at], sems.at[k]) for k in range(count) for at in [pl.ds(k * step, step)]]
    for copy in copies:
        copy.start()
    for copy in copies:
        copy.wait()


VMEM = pl.BlockSpec(memory_space=pltpu.VMEM)
SMEM = pl.BlockSpec(memory_space=pltpu.SMEM)


def on_chip(kernel, out_shape, nscalar, *args, limit=8 << 20):
    outs = pl.pallas_call(
        kernel,
        out_shape=out_shape,
        in_specs=[SMEM] * nscalar + [VMEM] * (len(args) - nscalar),
        out_specs=[VMEM] * len(out_shape),
        compiler_params=pltpu.CompilerParams(vmem_limit_bytes=limit),
    )(*args)
    return list(outs)


def loaded(array, count):
    held = pl.pallas_call(
        load_kernel,
        out_shape=pltpu.VMEM(array.shape, array.dtype),
        in_specs=[pl.BlockSpec(memory_space=pltpu.HBM)],
        out_specs=VMEM,
        scratch_shapes=[pltpu.SemaphoreType.DMA((count,))],
        compiler_params=pltpu.CompilerParams(vmem_limit_bytes=1 << 20),
    )(pltpu.with_memory_space_constraint(array, pltpu.HBM))
    return pltpu.with_memory_space_constraint(held, pltpu.VMEM)


def within(half):
    return sorted(range(1, half), key=lambda r: (-r.bit_count(), r))


def paired_body(amat, lam, hdiag, left_ops, right_operators, couple, blockmask):
    rows, width = amat.shape
    nsector = couple.shape[2]
    devices = lax.axis_size("ops")
    half = devices // 2
    inside = within(half)
    place = lax.axis_index("ops").astype(jnp.int32).reshape(1)
    shape = jax.ShapeDtypeStruct
    tile = shape((8, width), jnp.float32)
    sent, kept = shape((rows, width), jnp.bfloat16), shape((rows, width), jnp.float32)
    tailed = shape((rows + TAIL, width), jnp.bfloat16)

    def exchange(array, by):
        return lax.ppermute(array, "ops", [(o, o ^ by) for o in range(devices)])

    def gather(piece):
        pieces = {0: piece, half: exchange(piece, half)}
        for r in inside:
            pieces[r] = exchange(piece, r)
        for r in inside:
            pieces[half ^ r] = exchange(pieces[half], r)
        return pieces

    def apply_terms(pieces, left, right, dots):
        across = [half ^ r for r in inside]
        soon = inside.index(1)
        late = [t for t in range(len(inside)) if t != soon]
        whole = shape((devices * rows + width, width), jnp.bfloat16)
        fixed = (place, links, left, right)
        vector, *lead = on_chip(
            partial(first_kernel, list(pieces), across, dots),
            [whole] + [sent] * len(across) + [tile] * dots,
            2, *fixed, *pieces.values(),
        )
        outs = on_chip(
            partial(last_kernel, inside + [half, 0], dots),
            [sent] * len(inside) + [kept] * 2 + [tile] * (2 * dots),
            2, *fixed, vector, *((hdiag, lead[-1]) if dots else ()),
        )
        ours, (crossing, own, *sums) = outs[: len(inside)], outs[len(inside) :]
        if dots:
            numer, denom = sums
            other = exchange(numer, half)
        came = [exchange(chunk, r) for r, chunk in zip(inside, lead)]
        crossing = on_chip(added_kernel, [sent], 0, crossing, *came)[0]
        theirs = exchange(crossing, half)
        if dots:
            both, *tails = on_chip(
                partial(tail_kernel, len(ours) - 1), [tile] + [tailed] * (len(ours) - 1), 0, numer, other, *(ours[t] for t in late)
            )
            beside = exchange(both, inside[soon])
            for t, message in zip(late, tails):
                ours[t] = message
            sums = [both, beside, denom]
        ours = [exchange(chunk, r) for r, chunk in zip(inside, ours)]
        return [own, *ours, theirs], sums

    nterms = left_ops.shape[1]
    links = jnp.where(blockmask[0] != 0, couple[0], nsector).reshape(-1)
    place, links, left_ops, right_operators = lax.optimization_barrier((place, links, left_ops, right_operators))
    left = loaded(left_ops[0], nterms)
    right = loaded(right_operators[0], nterms)
    earlier = shifted(lam, "seg", 1)
    weights = jnp.where(lax.axis_index("seg") == 0, jnp.ones_like(earlier), earlier).reshape(-1, width)
    held = loaded(amat, 1)
    psi = on_chip(weigh_kernel, [sent], 0, weights, held)[0]
    terms, sums = apply_terms(gather(psi), left, right, True)
    correction, theta = on_chip(partial(correct_kernel, half), [sent, tile], 0, *terms, psi, hdiag, *sums)
    terms, _ = apply_terms(gather(correction), left, right, False)
    sigma_two = on_chip(final_kernel, [kept], 0, terms[0], correction, hdiag, *terms[1:])[0]
    return (sigma_two, theta[0, :1])


def is_paired(devices, nsector):
    return devices >= 4 and devices & (devices - 1) == 0 and nsector % devices == 0


def body(amat, lam, hdiag, left_ops, right_operators, couple, blockmask):
    form = paired_body if is_paired(lax.axis_size("ops"), couple.shape[2]) else gathered_body
    return form(amat, lam, hdiag, left_ops, right_operators, couple, blockmask)


def solution(mesh):
    placed = (
        P(("seg", "ops"), None),
        P(("seg", "ops")),
        P(("seg", "ops"), None),
        P("seg", "ops", None, None),
        P("seg", "ops", None, None),
        P("seg", "ops", None),
        P("seg", "ops", None),
    )
    return jax.shard_map(
        body,
        mesh=mesh,
        in_specs=placed,
        out_specs=(P(("seg", "ops"), None), P("seg")),
        check_vma=False,
    )
```

```python
from functools import partial

import jax
import jax.numpy as jnp
from jax import lax
from jax.experimental import pallas as pl
from jax.experimental.pallas import tpu as pltpu
from jax.sharding import PartitionSpec as P


def shifted(array, axis, by):
    devices = lax.axis_size(axis)
    pairs = [(i, i + by) for i in range(devices) if 0 <= i + by < devices]
    return lax.ppermute(array, axis, pairs)


def row_per_term(blocks, left, right, links, live, width, count):
    nterms = left.shape[0]
    nblock = count // width
    lrows = left.reshape(nterms, nblock, width, width)
    rblock = right.reshape(nterms, nblock, width, width)
    picked = blocks[links]
    inner_block = jnp.einsum("knra,knab->knrb", lrows, picked, preferred_element_type=jnp.float32)
    inner_block = (inner_block * live[:, :, None, None]).astype(jnp.bfloat16)
    result = jnp.einsum("knrb,kndb->nrd", inner_block, rblock, preferred_element_type=jnp.float32)
    return result.reshape(count, width)


def gathered_body(amat, lam, hdiag, left_ops, right_operators, couple, blockmask):
    width = amat.shape[1]
    links = couple[0]
    nsector = links.shape[1]
    bond = width * nsector
    live = blockmask[0].astype(jnp.float32)
    earlier = shifted(lam, "seg", 1)
    weights = jnp.where(lax.axis_index("seg") == 0, jnp.ones_like(earlier), earlier)
    psi = (weights[:, None] * amat.astype(jnp.float32)).astype(jnp.bfloat16)

    def apply_terms(vector):
        whole = lax.all_gather(vector, "ops", axis=0, tiled=True)
        blocks = whole.reshape(nsector, width, width)
        part = row_per_term(blocks, left_ops[0], right_operators[0], links, live, width, bond)
        summed = lax.psum_scatter(part, "ops", scatter_dimension=0, tiled=True)
        return summed + hdiag * vector.astype(jnp.float32)

    sigma_one = apply_terms(psi)
    psi_float = psi.astype(jnp.float32)
    numer, denom = lax.psum((jnp.sum(psi_float * sigma_one), jnp.sum(psi_float * psi_float)), "ops")
    quotient = numer / denom
    correction = ((sigma_one - quotient * psi_float) / hdiag).astype(jnp.bfloat16)
    sigma_two = apply_terms(correction)
    return (sigma_two, quotient.reshape(1))


def scaled_products(vector, links, left, right, chunks, per, packed, store):
    width = vector.shape[1]
    nsector = vector.shape[0] // width - 1
    nterms = left.shape[0]

    def inner_of(i, t, place):
        rows = pl.ds((t * per + place) * width if packed else pl.multiple_of(i * width, width), width)
        blocks = []
        for k in range(nterms):
            at = pl.multiple_of(links[k * nsector + i] * width, width)
            product = jnp.dot(left[k, rows, :], vector[pl.ds(at, width), :], preferred_element_type=jnp.float32)
            blocks.append(product.astype(jnp.bfloat16))
        return jnp.concatenate(blocks, axis=1), rows

    def outer_of(inner, rows):
        factors = jnp.concatenate([right[k, rows, :] for k in range(nterms)], axis=1)
        return lax.dot_general(inner, factors, (((1,), (1,)), ((), ())), preferred_element_type=jnp.float32)

    waiting = None
    for t, chunk in enumerate(chunks):
        for i in range(per):
            now = inner_of(chunk * per + i, t, i)
            if waiting is not None:
                store(*waiting[:2], outer_of(*waiting[2]))
            waiting = (t, i, now)
    store(*waiting[:2], outer_of(*waiting[2]))


def rows_at(chunk, rows):
    return pl.ds(pl.multiple_of(chunk * rows, rows), rows)


def squares(total, own):
    return jnp.sum((total * own).reshape(-1, 8, total.shape[1]), axis=0)


TAIL = 16


def chunk_sums(offsets, rows, place, links, left, right, vector, outs, numer, packed=False):
    width = vector.shape[1]
    chunks = [place[0] ^ offset for offset in offsets]

    def store(t, i, sums):
        at = slice(i * width, (i + 1) * width)
        outs[t][at, :] = sums.astype(outs[t].dtype)
        if numer is not None:
            start = pl.multiple_of(chunks[t] * rows + i * width, width)
            numer[...] += squares(sums, vector[pl.ds(start, width), :].astype(jnp.float32))

    scaled_products(vector, links, left, right, chunks, rows // width, packed, store)


def first_kernel(offsets, first, dots, place, links, left, right, *refs):
    npiece = len(offsets)
    pieces, vector, outs = refs[:npiece], refs[npiece], refs[npiece + 1 :]
    rows, width = pieces[0].shape
    for piece, offset in zip(pieces, offsets):
        vector[rows_at(place[0] ^ offset, rows), :] = piece[...]
    vector[npiece * rows :, :] = jnp.zeros((width, width), vector.dtype)
    numer = outs[-1] if dots else None
    if dots:
        numer[...] = jnp.zeros_like(numer)
    chunk_sums(first, rows, place, links, left, right, vector, outs, numer, packed=True)


def last_kernel(offsets, dots, place, links, left, right, vector, *refs):
    width = vector.shape[1]
    numer = None
    rows = refs[-1].shape[0]
    if dots:
        hdiag, before, *refs, numer, denom = refs
        rows = hdiag.shape[0]
        own = vector[rows_at(place[0], rows), :].astype(jnp.float32)
        numer[...] = before[...] + squares(hdiag[...] * own, own)
        whole = vector[: vector.shape[0] - width, :].astype(jnp.float32)
        denom[...] = squares(whole, whole)
    chunk_sums(offsets, rows, place, links, left, right, vector, refs, numer)


def three_roundings(part):
    row = lax.broadcasted_iota(jnp.int32, (TAIL, part.shape[1]), 0)
    tail = jnp.zeros((TAIL, part.shape[1]), jnp.float32)
    for r in range(3):
        rounded = part.astype(jnp.bfloat16).astype(jnp.float32)
        tail = jnp.where(row == r, rounded, tail)
        part = part - rounded
    return tail.astype(jnp.bfloat16)


def plus_kernel(mine, other, out):
    out[...] = mine[...] + other[...]


def tail_kernel(chunk, part, out):
    rows = chunk.shape[0]
    out[:rows, :] = chunk[...]
    out[rows:, :] = three_roundings(jnp.sum(part[...], axis=0, keepdims=True))


def added_kernel(kept, *refs):
    out = refs[-1]
    total = kept[...]
    for came in refs[:-1]:
        total = total + came[...].astype(jnp.float32)
    out[...] = total.astype(out.dtype)


def final_kernel(kept, vector, hdiag, *refs):
    out = refs[-1]
    total = kept[...] + hdiag[...] * vector[...].astype(jnp.float32)
    for came in refs[:-1]:
        total = total + came[...].astype(jnp.float32)
    out[...] = total


def correct_kernel(nmore, *refs):
    kept, more, refs = refs[0], refs[1 : 1 + nmore], refs[1 + nmore :]
    psi, hdiag, part, denom, correction, theta = refs
    rows = psi.shape[0]
    total = kept[...]
    numer = jnp.sum(part[...], keepdims=True)
    for m in more:
        total = total + m[:rows, :].astype(jnp.float32)
        if m.shape[0] > rows:
            numer = numer + jnp.sum(m[rows:, :].astype(jnp.float32), keepdims=True)
    quotient = numer / jnp.sum(denom[...], keepdims=True)
    vector = psi[...].astype(jnp.float32)
    sigma = total + hdiag[...] * vector
    correction[...] = ((sigma - quotient * vector) / hdiag[...]).astype(correction.dtype)
    theta[...] = jnp.broadcast_to(quotient, theta.shape)


def weigh_kernel(weights, piece, out):
    width = out.shape[1]
    columns = weights[...].T
    for i in range(weights.shape[0]):
        at = slice(i * width, (i + 1) * width)
        out[at, :] = (columns[:, i : i + 1] * piece[at, :].astype(jnp.float32)).astype(out.dtype)


def load_kernel(source, target, sems):
    count = sems.shape[0]
    step = source.shape[0] // count
    copies = [pltpu.make_async_copy(source.at[at], target.at[at], sems.at[k]) for k in range(count) for at in [pl.ds(k * step, step)]]
    for copy in copies:
        copy.start()
    for copy in copies:
        copy.wait()


def load_chunks_kernel(offsets, place, source, target, sems):
    rows = target.shape[1] // len(offsets)
    copies = [
        pltpu.make_async_copy(source.at[:, rows_at(place[0] ^ offset, rows)], target.at[:, pl.ds(t * rows, rows)], sems.at[t])
        for t, offset in enumerate(offsets)
    ]
    for copy in copies:
        copy.start()
    for copy in copies:
        copy.wait()


VMEM = pl.BlockSpec(memory_space=pltpu.VMEM)
SMEM = pl.BlockSpec(memory_space=pltpu.SMEM)


def on_chip(kernel, out_shape, nscalar, *args, limit=8 << 20):
    outs = pl.pallas_call(
        kernel,
        out_shape=out_shape,
        in_specs=[SMEM] * nscalar + [VMEM] * (len(args) - nscalar),
        out_specs=[VMEM] * len(out_shape),
        compiler_params=pltpu.CompilerParams(vmem_limit_bytes=limit),
    )(*args)
    return list(outs)


def loaded(array, count):
    held = pl.pallas_call(
        load_kernel,
        out_shape=pltpu.VMEM(array.shape, array.dtype),
        in_specs=[pl.BlockSpec(memory_space=pltpu.HBM)],
        out_specs=VMEM,
        scratch_shapes=[pltpu.SemaphoreType.DMA((count,))],
        compiler_params=pltpu.CompilerParams(vmem_limit_bytes=1 << 20),
    )(pltpu.with_memory_space_constraint(array, pltpu.HBM))
    return pltpu.with_memory_space_constraint(held, pltpu.VMEM)


def loaded_chunks(place, operators, offsets, rows):
    nterms, _, width = operators.shape
    held = pl.pallas_call(
        partial(load_chunks_kernel, offsets),
        out_shape=pltpu.VMEM((nterms, len(offsets) * rows, width), operators.dtype),
        in_specs=[SMEM, pl.BlockSpec(memory_space=pltpu.HBM)],
        out_specs=VMEM,
        scratch_shapes=[pltpu.SemaphoreType.DMA((len(offsets),))],
        compiler_params=pltpu.CompilerParams(vmem_limit_bytes=1 << 20),
    )(place, pltpu.with_memory_space_constraint(operators, pltpu.HBM))
    return pltpu.with_memory_space_constraint(held, pltpu.VMEM)


def within(half):
    return sorted(range(1, half), key=lambda r: (-r.bit_count(), r))


def paired_body(amat, lam, hdiag, left_ops, right_operators, couple, blockmask):
    rows, width = amat.shape
    nsector = couple.shape[2]
    devices = lax.axis_size("ops")
    half = devices // 2
    inside = within(half)
    place = lax.axis_index("ops").astype(jnp.int32).reshape(1)
    shape = jax.ShapeDtypeStruct
    tile = shape((8, width), jnp.float32)
    sent, kept = shape((rows, width), jnp.bfloat16), shape((rows, width), jnp.float32)
    tailed = shape((rows + TAIL, width), jnp.bfloat16)

    def exchange(array, by):
        return lax.ppermute(array, "ops", [(o, o ^ by) for o in range(devices)])

    def gather(piece):
        pieces = {0: piece, half: exchange(piece, half)}
        for r in inside:
            pieces[r] = exchange(piece, r)
        for r in inside:
            pieces[half ^ r] = exchange(pieces[half], r)
        return pieces

    def apply_terms(pieces, lead_left, left, lead_right, right, dots):
        across = [half ^ r for r in inside]
        whole = shape((devices * rows + width, width), jnp.bfloat16)
        vector, *lead = on_chip(
            partial(first_kernel, list(pieces), across, dots),
            [whole] + [sent] * len(across) + [tile] * dots,
            2, place, links, lead_left, lead_right, *pieces.values(),
        )
        outs = on_chip(
            partial(last_kernel, inside + [half, 0], dots),
            [sent] * len(inside) + [kept] * 2 + [tile] * (2 * dots),
            2, place, links, left, right, vector, *((hdiag, lead[-1]) if dots else ()),
        )
        ours, (crossing, own, *sums) = outs[: len(inside)], outs[len(inside) :]
        if dots:
            numer, denom = sums
            other = exchange(numer, half)
        came = [exchange(chunk, r) for r, chunk in zip(inside, lead)]
        crossing = on_chip(added_kernel, [sent], 0, crossing, *came)[0]
        theirs = exchange(crossing, half)
        if dots:
            part = on_chip(plus_kernel, [tile], 0, numer, other)[0]
            for b in [1 << b for b in range(half.bit_length() - 2)]:
                part = on_chip(plus_kernel, [tile], 0, part, exchange(part, b))[0]
            if inside:
                ours[-1] = on_chip(tail_kernel, [tailed], 0, ours[-1], part)[0]
            sums = [part, denom]
        ours = [exchange(chunk, r) for r, chunk in zip(inside, ours)]
        return [own, *ours, theirs], sums

    links = jnp.where(blockmask[0] != 0, couple[0], nsector).reshape(-1)
    place, links, left_ops, right_operators = lax.optimization_barrier((place, links, left_ops, right_operators))
    lead_left = loaded_chunks(place, left_ops[0], [half ^ r for r in inside], rows)
    left = pltpu.with_memory_space_constraint(left_ops[0], pltpu.VMEM)
    lead_right = loaded_chunks(place, right_operators[0], [half ^ r for r in inside], rows)
    right = pltpu.with_memory_space_constraint(right_operators[0], pltpu.VMEM)
    earlier = shifted(lam, "seg", 1)
    weights = jnp.where(lax.axis_index("seg") == 0, jnp.ones_like(earlier), earlier).reshape(-1, width)
    held = loaded(amat, 1)
    psi = on_chip(weigh_kernel, [sent], 0, weights, held)[0]
    terms, sums = apply_terms(gather(psi), lead_left, left, lead_right, right, True)
    correction, theta = on_chip(partial(correct_kernel, half), [sent, tile], 0, *terms, psi, hdiag, *sums)
    terms, _ = apply_terms(gather(correction), lead_left, left, lead_right, right, False)
    sigma_two = on_chip(final_kernel, [kept], 0, terms[0], correction, hdiag, *terms[1:])[0]
    return (sigma_two, theta[0, :1])


def is_paired(devices, nsector):
    return devices >= 4 and devices & (devices - 1) == 0 and nsector % devices == 0


def body(amat, lam, hdiag, left_ops, right_operators, couple, blockmask):
    form = paired_body if is_paired(lax.axis_size("ops"), couple.shape[2]) else gathered_body
    return form(amat, lam, hdiag, left_ops, right_operators, couple, blockmask)


def solution(mesh):
    placed = (
        P(("seg", "ops"), None),
        P(("seg", "ops")),
        P(("seg", "ops"), None),
        P("seg", "ops", None, None),
        P("seg", "ops", None, None),
        P("seg", "ops", None),
        P("seg", "ops", None),
    )
    return jax.shard_map(
        body,
        mesh=mesh,
        in_specs=placed,
        out_specs=(P(("seg", "ops"), None), P("seg")),
        check_vma=False,
    )
```

```python
from functools import partial

import jax
import jax.numpy as jnp
from jax import lax
from jax.experimental import pallas as pl
from jax.experimental.pallas import tpu as pltpu
from jax.sharding import PartitionSpec as P


def shifted(array, axis, by):
    devices = lax.axis_size(axis)
    pairs = [(i, i + by) for i in range(devices) if 0 <= i + by < devices]
    return lax.ppermute(array, axis, pairs)


def row_per_term(blocks, left, right, links, live, width, count):
    nterms = left.shape[0]
    nblock = count // width
    lrows = left.reshape(nterms, nblock, width, width)
    rblock = right.reshape(nterms, nblock, width, width)
    picked = blocks[links]
    inner_block = jnp.einsum("knra,knab->knrb", lrows, picked, preferred_element_type=jnp.float32)
    inner_block = (inner_block * live[:, :, None, None]).astype(jnp.bfloat16)
    result = jnp.einsum("knrb,kndb->nrd", inner_block, rblock, preferred_element_type=jnp.float32)
    return result.reshape(count, width)


def gathered_body(amat, lam, hdiag, left_ops, right_operators, couple, blockmask):
    width = amat.shape[1]
    links = couple[0]
    nsector = links.shape[1]
    bond = width * nsector
    live = blockmask[0].astype(jnp.float32)
    earlier = shifted(lam, "seg", 1)
    weights = jnp.where(lax.axis_index("seg") == 0, jnp.ones_like(earlier), earlier)
    psi = (weights[:, None] * amat.astype(jnp.float32)).astype(jnp.bfloat16)

    def apply_terms(vector):
        whole = lax.all_gather(vector, "ops", axis=0, tiled=True)
        blocks = whole.reshape(nsector, width, width)
        part = row_per_term(blocks, left_ops[0], right_operators[0], links, live, width, bond)
        summed = lax.psum_scatter(part, "ops", scatter_dimension=0, tiled=True)
        return summed + hdiag * vector.astype(jnp.float32)

    sigma_one = apply_terms(psi)
    psi_float = psi.astype(jnp.float32)
    numer, denom = lax.psum((jnp.sum(psi_float * sigma_one), jnp.sum(psi_float * psi_float)), "ops")
    quotient = numer / denom
    correction = ((sigma_one - quotient * psi_float) / hdiag).astype(jnp.bfloat16)
    sigma_two = apply_terms(correction)
    return (sigma_two, quotient.reshape(1))


def scaled_products(vector, links, left, right, chunks, per, packed, store):
    width = vector.shape[1]
    nsector = vector.shape[0] // width - 1
    nterms = left.shape[0]

    def inner_of(i, t, place):
        rows = pl.ds((t * per + place) * width if packed else pl.multiple_of(i * width, width), width)
        blocks = []
        for k in range(nterms):
            at = pl.multiple_of(links[k * nsector + i] * width, width)
            product = jnp.dot(left[k, rows, :], vector[pl.ds(at, width), :], preferred_element_type=jnp.float32)
            blocks.append(product.astype(jnp.bfloat16))
        return jnp.concatenate(blocks, axis=1), rows

    def outer_of(inner, rows):
        factors = jnp.concatenate([right[k, rows, :] for k in range(nterms)], axis=1)
        return lax.dot_general(inner, factors, (((1,), (1,)), ((), ())), preferred_element_type=jnp.float32)

    waiting = None
    for t, chunk in enumerate(chunks):
        for i in range(per):
            now = inner_of(chunk * per + i, t, i)
            if waiting is not None:
                store(*waiting[:2], outer_of(*waiting[2]))
            waiting = (t, i, now)
    store(*waiting[:2], outer_of(*waiting[2]))


def rows_at(chunk, rows):
    return pl.ds(pl.multiple_of(chunk * rows, rows), rows)


def squares(total, own):
    return jnp.sum((total * own).reshape(-1, 8, total.shape[1]), axis=0)


TAIL = 16


def chunk_sums(offsets, rows, place, links, left, right, vector, outs, numer, packed=False):
    width = vector.shape[1]
    chunks = [place[0] ^ offset for offset in offsets]

    def store(t, i, sums):
        at = slice(i * width, (i + 1) * width)
        outs[t][at, :] = sums.astype(outs[t].dtype)
        if numer is not None:
            start = pl.multiple_of(chunks[t] * rows + i * width, width)
            numer[...] += squares(sums, vector[pl.ds(start, width), :].astype(jnp.float32))

    scaled_products(vector, links, left, right, chunks, rows // width, packed, store)


def lay_kernel(offsets, place, *refs):
    vector = refs[-1]
    rows, width = refs[0].shape
    for piece, offset in zip(refs[:-1], offsets):
        vector[rows_at(place[0] ^ offset, rows), :] = piece[...]
    vector[vector.shape[0] - width :, :] = jnp.zeros((width, width), vector.dtype)


def first_kernel(offsets, first, dots, place, links, left, right, *refs):
    npiece = len(offsets)
    pieces, vector, outs = refs[:npiece], refs[npiece + 1], refs[npiece + 2 :]
    rows = outs[0].shape[0]
    for piece, offset in zip(pieces, offsets):
        vector[rows_at(place[0] ^ offset, rows), :] = piece[...]
    numer = outs[-1] if dots else None
    if dots:
        numer[...] = jnp.zeros_like(numer)
    chunk_sums(first, rows, place, links, left, right, vector, outs, numer, packed=True)


def last_kernel(offsets, dots, place, links, left, right, vector, *refs):
    width = vector.shape[1]
    numer = None
    rows = refs[-1].shape[0]
    if dots:
        hdiag, before, *refs, numer, denom = refs
        rows = hdiag.shape[0]
        own = vector[rows_at(place[0], rows), :].astype(jnp.float32)
        numer[...] = before[...] + squares(hdiag[...] * own, own)
        whole = vector[: vector.shape[0] - width, :].astype(jnp.float32)
        denom[...] = squares(whole, whole)
    chunk_sums(offsets, rows, place, links, left, right, vector, refs, numer)


def three_roundings(part):
    row = lax.broadcasted_iota(jnp.int32, (TAIL, part.shape[1]), 0)
    tail = jnp.zeros((TAIL, part.shape[1]), jnp.float32)
    for r in range(3):
        rounded = part.astype(jnp.bfloat16).astype(jnp.float32)
        tail = jnp.where(row == r, rounded, tail)
        part = part - rounded
    return tail.astype(jnp.bfloat16)


def plus_kernel(mine, other, out):
    out[...] = mine[...] + other[...]


def tail_kernel(chunk, part, out):
    rows = chunk.shape[0]
    out[:rows, :] = chunk[...]
    out[rows:, :] = three_roundings(jnp.sum(part[...], axis=0, keepdims=True))


def added_kernel(kept, *refs):
    out = refs[-1]
    total = kept[...]
    for came in refs[:-1]:
        total = total + came[...].astype(jnp.float32)
    out[...] = total.astype(out.dtype)


def final_kernel(kept, vector, hdiag, *refs):
    out = refs[-1]
    total = kept[...] + hdiag[...] * vector[...].astype(jnp.float32)
    for came in refs[:-1]:
        total = total + came[...].astype(jnp.float32)
    out[...] = total


def correct_kernel(nmore, *refs):
    kept, more, refs = refs[0], refs[1 : 1 + nmore], refs[1 + nmore :]
    psi, hdiag, part, denom, correction, theta = refs
    rows = psi.shape[0]
    total = kept[...]
    numer = jnp.sum(part[...], keepdims=True)
    for m in more:
        total = total + m[:rows, :].astype(jnp.float32)
        if m.shape[0] > rows:
            numer = numer + jnp.sum(m[rows:, :].astype(jnp.float32), keepdims=True)
    quotient = numer / jnp.sum(denom[...], keepdims=True)
    vector = psi[...].astype(jnp.float32)
    sigma = total + hdiag[...] * vector
    correction[...] = ((sigma - quotient * vector) / hdiag[...]).astype(correction.dtype)
    theta[...] = jnp.broadcast_to(quotient, theta.shape)


def weigh_kernel(weights, piece, out):
    width = out.shape[1]
    columns = weights[...].T
    for i in range(weights.shape[0]):
        at = slice(i * width, (i + 1) * width)
        out[at, :] = (columns[:, i : i + 1] * piece[at, :].astype(jnp.float32)).astype(out.dtype)


def load_kernel(source, target, sems):
    count = sems.shape[0]
    step = source.shape[0] // count
    copies = [pltpu.make_async_copy(source.at[at], target.at[at], sems.at[k]) for k in range(count) for at in [pl.ds(k * step, step)]]
    for copy in copies:
        copy.start()
    for copy in copies:
        copy.wait()


def load_chunks_kernel(offsets, place, source, target, sems):
    rows = target.shape[1] // len(offsets)
    copies = [
        pltpu.make_async_copy(source.at[:, rows_at(place[0] ^ offset, rows)], target.at[:, pl.ds(t * rows, rows)], sems.at[t])
        for t, offset in enumerate(offsets)
    ]
    for copy in copies:
        copy.start()
    for copy in copies:
        copy.wait()


VMEM = pl.BlockSpec(memory_space=pltpu.VMEM)
SMEM = pl.BlockSpec(memory_space=pltpu.SMEM)


def on_chip(kernel, out_shape, nscalar, *args, limit=8 << 20, aliases={}):
    outs = pl.pallas_call(
        kernel,
        out_shape=out_shape,
        in_specs=[SMEM] * nscalar + [VMEM] * (len(args) - nscalar),
        out_specs=[VMEM] * len(out_shape),
        input_output_aliases=aliases,
        compiler_params=pltpu.CompilerParams(vmem_limit_bytes=limit),
    )(*args)
    return list(outs)


def loaded(array, count):
    held = pl.pallas_call(
        load_kernel,
        out_shape=pltpu.VMEM(array.shape, array.dtype),
        in_specs=[pl.BlockSpec(memory_space=pltpu.HBM)],
        out_specs=VMEM,
        scratch_shapes=[pltpu.SemaphoreType.DMA((count,))],
        compiler_params=pltpu.CompilerParams(vmem_limit_bytes=1 << 20),
    )(pltpu.with_memory_space_constraint(array, pltpu.HBM))
    return pltpu.with_memory_space_constraint(held, pltpu.VMEM)


def loaded_chunks(place, operators, offsets, rows):
    nterms, _, width = operators.shape
    held = pl.pallas_call(
        partial(load_chunks_kernel, offsets),
        out_shape=pltpu.VMEM((nterms, len(offsets) * rows, width), operators.dtype),
        in_specs=[SMEM, pl.BlockSpec(memory_space=pltpu.HBM)],
        out_specs=VMEM,
        scratch_shapes=[pltpu.SemaphoreType.DMA((len(offsets),))],
        compiler_params=pltpu.CompilerParams(vmem_limit_bytes=1 << 20),
    )(place, pltpu.with_memory_space_constraint(operators, pltpu.HBM))
    return pltpu.with_memory_space_constraint(held, pltpu.VMEM)


def within(half):
    return sorted(range(1, half), key=lambda r: (-r.bit_count(), r))


def paired_body(amat, lam, hdiag, left_ops, right_operators, couple, blockmask):
    rows, width = amat.shape
    nsector = couple.shape[2]
    devices = lax.axis_size("ops")
    half = devices // 2
    inside = within(half)
    place = lax.axis_index("ops").astype(jnp.int32).reshape(1)
    shape = jax.ShapeDtypeStruct
    tile = shape((8, width), jnp.float32)
    sent, kept = shape((rows, width), jnp.bfloat16), shape((rows, width), jnp.float32)
    tailed = shape((rows + TAIL, width), jnp.bfloat16)

    def exchange(array, by):
        return lax.ppermute(array, "ops", [(o, o ^ by) for o in range(devices)])

    def gather(piece):
        pieces = {0: piece, half: exchange(piece, half)}
        for r in inside:
            pieces[r] = exchange(piece, r)
        for r in inside:
            pieces[half ^ r] = exchange(pieces[half], r)
        return pieces

    def apply_terms(pieces, lead_left, left, lead_right, right, dots):
        across = [half ^ r for r in inside]
        whole = shape((devices * rows + width, width), jnp.bfloat16)
        early, late = list(pieces)[: len(pieces) - len(inside)], list(pieces)[len(pieces) - len(inside) :]
        laid = on_chip(partial(lay_kernel, early), [whole], 1, place, *(pieces[p] for p in early))[0]
        vector, *lead = on_chip(
            partial(first_kernel, late, across, dots),
            [whole] + [sent] * len(across) + [tile] * dots,
            2, place, links, lead_left, lead_right, *(pieces[p] for p in late), laid,
            aliases={4 + len(late): 0},
        )
        outs = on_chip(
            partial(last_kernel, inside + [half, 0], dots),
            [sent] * len(inside) + [kept] * 2 + [tile] * (2 * dots),
            2, place, links, left, right, vector, *((hdiag, lead[-1]) if dots else ()),
        )
        ours, (crossing, own, *sums) = outs[: len(inside)], outs[len(inside) :]
        if dots:
            numer, denom = sums
            other = exchange(numer, half)
        came = [exchange(chunk, r) for r, chunk in zip(inside, lead)]
        crossing = on_chip(added_kernel, [sent], 0, crossing, *came)[0]
        theirs = exchange(crossing, half)
        if dots:
            part = on_chip(plus_kernel, [tile], 0, numer, other)[0]
            for b in [1 << b for b in range(half.bit_length() - 2)]:
                part = on_chip(plus_kernel, [tile], 0, part, exchange(part, b))[0]
            if inside:
                ours[-1] = on_chip(tail_kernel, [tailed], 0, ours[-1], part)[0]
            sums = [part, denom]
        ours = [exchange(chunk, r) for r, chunk in zip(inside, ours)]
        return [own, *ours, theirs], sums

    links = jnp.where(blockmask[0] != 0, couple[0], nsector).reshape(-1)
    place, links, left_ops, right_operators = lax.optimization_barrier((place, links, left_ops, right_operators))
    lead_left = loaded_chunks(place, left_ops[0], [half ^ r for r in inside], rows)
    left = pltpu.with_memory_space_constraint(left_ops[0], pltpu.VMEM)
    lead_right = loaded_chunks(place, right_operators[0], [half ^ r for r in inside], rows)
    right = pltpu.with_memory_space_constraint(right_operators[0], pltpu.VMEM)
    earlier = shifted(lam, "seg", 1)
    weights = jnp.where(lax.axis_index("seg") == 0, jnp.ones_like(earlier), earlier).reshape(-1, width)
    held = loaded(amat, 1)
    psi = on_chip(weigh_kernel, [sent], 0, weights, held)[0]
    terms, sums = apply_terms(gather(psi), lead_left, left, lead_right, right, True)
    correction, theta = on_chip(partial(correct_kernel, half), [sent, tile], 0, *terms, psi, hdiag, *sums)
    terms, _ = apply_terms(gather(correction), lead_left, left, lead_right, right, False)
    sigma_two = on_chip(final_kernel, [kept], 0, terms[0], correction, hdiag, *terms[1:])[0]
    return (sigma_two, theta[0, :1])


def is_paired(devices, nsector):
    return devices >= 4 and devices & (devices - 1) == 0 and nsector % devices == 0


def body(amat, lam, hdiag, left_ops, right_operators, couple, blockmask):
    form = paired_body if is_paired(lax.axis_size("ops"), couple.shape[2]) else gathered_body
    return form(amat, lam, hdiag, left_ops, right_operators, couple, blockmask)


def solution(mesh):
    placed = (
        P(("seg", "ops"), None),
        P(("seg", "ops")),
        P(("seg", "ops"), None),
        P("seg", "ops", None, None),
        P("seg", "ops", None, None),
        P("seg", "ops", None),
        P("seg", "ops", None),
    )
    return jax.shard_map(
        body,
        mesh=mesh,
        in_specs=placed,
        out_specs=(P(("seg", "ops"), None), P("seg")),
        check_vma=False,
    )
```

```python
from functools import partial

import jax
import jax.numpy as jnp
from jax import lax
from jax.experimental import pallas as pl
from jax.experimental.pallas import tpu as pltpu
from jax.sharding import PartitionSpec as P


def shifted(array, axis, by):
    devices = lax.axis_size(axis)
    pairs = [(i, i + by) for i in range(devices) if 0 <= i + by < devices]
    return lax.ppermute(array, axis, pairs)


def row_per_term(blocks, left, right, links, live, width, count):
    nterms = left.shape[0]
    nblock = count // width
    lrows = left.reshape(nterms, nblock, width, width)
    rblock = right.reshape(nterms, nblock, width, width)
    picked = blocks[links]
    inner_block = jnp.einsum("knra,knab->knrb", lrows, picked, preferred_element_type=jnp.float32)
    inner_block = (inner_block * live[:, :, None, None]).astype(jnp.bfloat16)
    result = jnp.einsum("knrb,kndb->nrd", inner_block, rblock, preferred_element_type=jnp.float32)
    return result.reshape(count, width)


def gathered_body(amat, lam, hdiag, left_ops, right_operators, couple, blockmask):
    width = amat.shape[1]
    links = couple[0]
    nsector = links.shape[1]
    bond = width * nsector
    live = blockmask[0].astype(jnp.float32)
    earlier = shifted(lam, "seg", 1)
    weights = jnp.where(lax.axis_index("seg") == 0, jnp.ones_like(earlier), earlier)
    psi = (weights[:, None] * amat.astype(jnp.float32)).astype(jnp.bfloat16)

    def apply_terms(vector):
        whole = lax.all_gather(vector, "ops", axis=0, tiled=True)
        blocks = whole.reshape(nsector, width, width)
        part = row_per_term(blocks, left_ops[0], right_operators[0], links, live, width, bond)
        summed = lax.psum_scatter(part, "ops", scatter_dimension=0, tiled=True)
        return summed + hdiag * vector.astype(jnp.float32)

    sigma_one = apply_terms(psi)
    psi_float = psi.astype(jnp.float32)
    numer, denom = lax.psum((jnp.sum(psi_float * sigma_one), jnp.sum(psi_float * psi_float)), "ops")
    quotient = numer / denom
    correction = ((sigma_one - quotient * psi_float) / hdiag).astype(jnp.bfloat16)
    sigma_two = apply_terms(correction)
    return (sigma_two, quotient.reshape(1))


def scaled_products(vector, links, left, right, chunks, per, packed, store):
    width = vector.shape[1]
    nsector = vector.shape[0] // width - 1
    nterms = left.shape[0]

    def inner_of(i, t, place):
        rows = pl.ds((t * per + place) * width if packed else pl.multiple_of(i * width, width), width)
        blocks = []
        for k in range(nterms):
            at = pl.multiple_of(links[k * nsector + i] * width, width)
            product = jnp.dot(left[k, rows, :], vector[pl.ds(at, width), :], preferred_element_type=jnp.float32)
            blocks.append(product.astype(jnp.bfloat16))
        return jnp.concatenate(blocks, axis=1), rows

    def outer_of(inner, rows):
        factors = jnp.concatenate([right[k, rows, :] for k in range(nterms)], axis=1)
        return lax.dot_general(inner, factors, (((1,), (1,)), ((), ())), preferred_element_type=jnp.float32)

    waiting = None
    for t, chunk in enumerate(chunks):
        for i in range(per):
            now = inner_of(chunk * per + i, t, i)
            if waiting is not None:
                store(*waiting[:2], outer_of(*waiting[2]))
            waiting = (t, i, now)
    store(*waiting[:2], outer_of(*waiting[2]))


def rows_at(chunk, rows):
    return pl.ds(pl.multiple_of(chunk * rows, rows), rows)


def squares(total, own):
    return jnp.sum((total * own).reshape(-1, 8, total.shape[1]), axis=0)


TAIL = 16


def chunk_sums(offsets, rows, place, links, left, right, vector, outs, numer, packed=False):
    width = vector.shape[1]
    chunks = [place[0] ^ offset for offset in offsets]

    def store(t, i, sums):
        at = slice(i * width, (i + 1) * width)
        outs[t][at, :] = sums.astype(outs[t].dtype)
        if numer is not None:
            start = pl.multiple_of(chunks[t] * rows + i * width, width)
            numer[...] += squares(sums, vector[pl.ds(start, width), :].astype(jnp.float32))

    scaled_products(vector, links, left, right, chunks, rows // width, packed, store)


def lay_kernel(offsets, place, *refs):
    vector = refs[-1]
    rows, width = refs[0].shape
    for piece, offset in zip(refs[:-1], offsets):
        vector[rows_at(place[0] ^ offset, rows), :] = piece[...]
    vector[vector.shape[0] - width :, :] = jnp.zeros((width, width), vector.dtype)


def first_kernel(offsets, first, dots, place, links, left, right, *refs):
    npiece = len(offsets)
    pieces, vector, outs = refs[:npiece], refs[npiece + 1], refs[npiece + 2 :]
    rows = outs[0].shape[0]
    for piece, offset in zip(pieces, offsets):
        vector[rows_at(place[0] ^ offset, rows), :] = piece[...]
    numer = outs[-1] if dots else None
    if dots:
        numer[...] = jnp.zeros_like(numer)
    chunk_sums(first, rows, place, links, left, right, vector, outs, numer, packed=True)


def last_kernel(offsets, dots, place, links, left, right, vector, *refs):
    width = vector.shape[1]
    numer = None
    rows = refs[-1].shape[0]
    if dots:
        hdiag, before, *refs, numer, denom = refs
        rows = hdiag.shape[0]
        own = vector[rows_at(place[0], rows), :].astype(jnp.float32)
        numer[...] = before[...] + squares(hdiag[...] * own, own)
        whole = vector[: vector.shape[0] - width, :].astype(jnp.float32)
        denom[...] = squares(whole, whole)
    chunk_sums(offsets, rows, place, links, left, right, vector, refs, numer)


def three_roundings(part):
    row = lax.broadcasted_iota(jnp.int32, (TAIL, part.shape[1]), 0)
    tail = jnp.zeros((TAIL, part.shape[1]), jnp.float32)
    for r in range(3):
        rounded = part.astype(jnp.bfloat16).astype(jnp.float32)
        tail = jnp.where(row == r, rounded, tail)
        part = part - rounded
    return tail.astype(jnp.bfloat16)


def plus_kernel(mine, other, out):
    out[...] = mine[...] + other[...]


def tail_kernel(chunk, part, out):
    rows = chunk.shape[0]
    out[:rows, :] = chunk[...]
    out[rows:, :] = three_roundings(jnp.sum(part[...], axis=0, keepdims=True))


def added_kernel(kept, *refs):
    out = refs[-1]
    total = kept[...]
    for came in refs[:-1]:
        total = total + came[...].astype(jnp.float32)
    out[...] = total.astype(out.dtype)


def base_kernel(kept, vector, hdiag, out):
    out[...] = kept[...] + hdiag[...] * vector[...].astype(jnp.float32)


def final_kernel(base, *refs):
    out = refs[-1]
    total = base[...]
    for came in refs[:-1]:
        total = total + came[...].astype(jnp.float32)
    out[...] = total


def correct_kernel(nmore, *refs):
    kept, more, refs = refs[0], refs[1 : 1 + nmore], refs[1 + nmore :]
    psi, hdiag, part, denom, correction, theta = refs
    rows = psi.shape[0]
    total = kept[...]
    numer = jnp.sum(part[...], keepdims=True)
    for m in more:
        total = total + m[:rows, :].astype(jnp.float32)
        if m.shape[0] > rows:
            numer = numer + jnp.sum(m[rows:, :].astype(jnp.float32), keepdims=True)
    quotient = numer / jnp.sum(denom[...], keepdims=True)
    vector = psi[...].astype(jnp.float32)
    sigma = total + hdiag[...] * vector
    correction[...] = ((sigma - quotient * vector) / hdiag[...]).astype(correction.dtype)
    theta[...] = jnp.broadcast_to(quotient, theta.shape)


def weigh_kernel(weights, piece, out):
    width = out.shape[1]
    columns = weights[...].T
    for i in range(weights.shape[0]):
        at = slice(i * width, (i + 1) * width)
        out[at, :] = (columns[:, i : i + 1] * piece[at, :].astype(jnp.float32)).astype(out.dtype)


def load_kernel(source, target, sems):
    count = sems.shape[0]
    step = source.shape[0] // count
    copies = [pltpu.make_async_copy(source.at[at], target.at[at], sems.at[k]) for k in range(count) for at in [pl.ds(k * step, step)]]
    for copy in copies:
        copy.start()
    for copy in copies:
        copy.wait()


def load_chunks_kernel(offsets, place, source, target, sems):
    rows = target.shape[1] // len(offsets)
    copies = [
        pltpu.make_async_copy(source.at[:, rows_at(place[0] ^ offset, rows)], target.at[:, pl.ds(t * rows, rows)], sems.at[t])
        for t, offset in enumerate(offsets)
    ]
    for copy in copies:
        copy.start()
    for copy in copies:
        copy.wait()


VMEM = pl.BlockSpec(memory_space=pltpu.VMEM)
SMEM = pl.BlockSpec(memory_space=pltpu.SMEM)


def on_chip(kernel, out_shape, nscalar, *args, limit=8 << 20, aliases={}):
    outs = pl.pallas_call(
        kernel,
        out_shape=out_shape,
        in_specs=[SMEM] * nscalar + [VMEM] * (len(args) - nscalar),
        out_specs=[VMEM] * len(out_shape),
        input_output_aliases=aliases,
        compiler_params=pltpu.CompilerParams(vmem_limit_bytes=limit),
    )(*args)
    return list(outs)


def loaded(array, count):
    held = pl.pallas_call(
        load_kernel,
        out_shape=pltpu.VMEM(array.shape, array.dtype),
        in_specs=[pl.BlockSpec(memory_space=pltpu.HBM)],
        out_specs=VMEM,
        scratch_shapes=[pltpu.SemaphoreType.DMA((count,))],
        compiler_params=pltpu.CompilerParams(vmem_limit_bytes=1 << 20),
    )(pltpu.with_memory_space_constraint(array, pltpu.HBM))
    return pltpu.with_memory_space_constraint(held, pltpu.VMEM)


def loaded_chunks(place, operators, offsets, rows):
    nterms, _, width = operators.shape
    held = pl.pallas_call(
        partial(load_chunks_kernel, offsets),
        out_shape=pltpu.VMEM((nterms, len(offsets) * rows, width), operators.dtype),
        in_specs=[SMEM, pl.BlockSpec(memory_space=pltpu.HBM)],
        out_specs=VMEM,
        scratch_shapes=[pltpu.SemaphoreType.DMA((len(offsets),))],
        compiler_params=pltpu.CompilerParams(vmem_limit_bytes=1 << 20),
    )(place, pltpu.with_memory_space_constraint(operators, pltpu.HBM))
    return pltpu.with_memory_space_constraint(held, pltpu.VMEM)


def within(half):
    return sorted(range(1, half), key=lambda r: (-r.bit_count(), r))


def paired_body(amat, lam, hdiag, left_ops, right_operators, couple, blockmask):
    rows, width = amat.shape
    nsector = couple.shape[2]
    devices = lax.axis_size("ops")
    half = devices // 2
    inside = within(half)
    place = lax.axis_index("ops").astype(jnp.int32).reshape(1)
    shape = jax.ShapeDtypeStruct
    tile = shape((8, width), jnp.float32)
    sent, kept = shape((rows, width), jnp.bfloat16), shape((rows, width), jnp.float32)
    tailed = shape((rows + TAIL, width), jnp.bfloat16)

    def exchange(array, by):
        return lax.ppermute(array, "ops", [(o, o ^ by) for o in range(devices)])

    def gather(piece):
        pieces = {0: piece, half: exchange(piece, half)}
        for r in inside:
            pieces[r] = exchange(piece, r)
        for r in inside:
            pieces[half ^ r] = exchange(pieces[half], r)
        return pieces

    def apply_terms(pieces, lead_left, left, lead_right, right, dots):
        across = [half ^ r for r in inside]
        whole = shape((devices * rows + width, width), jnp.bfloat16)
        early, late = list(pieces)[: len(pieces) - len(inside)], list(pieces)[len(pieces) - len(inside) :]
        laid = on_chip(partial(lay_kernel, early), [whole], 1, place, *(pieces[p] for p in early))[0]
        vector, *lead = on_chip(
            partial(first_kernel, late, across, dots),
            [whole] + [sent] * len(across) + [tile] * dots,
            2, place, links, lead_left, lead_right, *(pieces[p] for p in late), laid,
            aliases={4 + len(late): 0},
        )
        outs = on_chip(
            partial(last_kernel, inside + [half, 0], dots),
            [sent] * len(inside) + [kept] * 2 + [tile] * (2 * dots),
            2, place, links, left, right, vector, *((hdiag, lead[-1]) if dots else ()),
        )
        ours, (crossing, own, *sums) = outs[: len(inside)], outs[len(inside) :]
        if dots:
            numer, denom = sums
            other = exchange(numer, half)
        came = [exchange(chunk, r) for r, chunk in zip(inside, lead)]
        crossing = on_chip(added_kernel, [sent], 0, crossing, *came)[0]
        theirs = exchange(crossing, half)
        if dots:
            part = on_chip(plus_kernel, [tile], 0, numer, other)[0]
            for b in [1 << b for b in range(half.bit_length() - 2)]:
                part = on_chip(plus_kernel, [tile], 0, part, exchange(part, b))[0]
            if inside:
                ours[-1] = on_chip(tail_kernel, [tailed], 0, ours[-1], part)[0]
            sums = [part, denom]
        ours = [exchange(chunk, r) for r, chunk in zip(inside, ours)]
        return [own, *ours, theirs], sums

    links = jnp.where(blockmask[0] != 0, couple[0], nsector).reshape(-1)
    place, links, left_ops, right_operators = lax.optimization_barrier((place, links, left_ops, right_operators))
    lead_left = loaded_chunks(place, left_ops[0], [half ^ r for r in inside], rows)
    left = pltpu.with_memory_space_constraint(left_ops[0], pltpu.VMEM)
    lead_right = loaded_chunks(place, right_operators[0], [half ^ r for r in inside], rows)
    right = pltpu.with_memory_space_constraint(right_operators[0], pltpu.VMEM)
    earlier = shifted(lam, "seg", 1)
    weights = jnp.where(lax.axis_index("seg") == 0, jnp.ones_like(earlier), earlier).reshape(-1, width)
    held = loaded(amat, 1)
    psi = on_chip(weigh_kernel, [sent], 0, weights, held)[0]
    terms, sums = apply_terms(gather(psi), lead_left, left, lead_right, right, True)
    correction, theta = on_chip(partial(correct_kernel, half), [sent, tile], 0, *terms, psi, hdiag, *sums)
    terms, _ = apply_terms(gather(correction), lead_left, left, lead_right, right, False)
    base = on_chip(base_kernel, [kept], 0, terms[0], correction, hdiag)[0]
    sigma_two = on_chip(final_kernel, [kept], 0, base, *terms[1:])[0]
    return (sigma_two, theta[0, :1])


def is_paired(devices, nsector):
    return devices >= 4 and devices & (devices - 1) == 0 and nsector % devices == 0


def body(amat, lam, hdiag, left_ops, right_operators, couple, blockmask):
    form = paired_body if is_paired(lax.axis_size("ops"), couple.shape[2]) else gathered_body
    return form(amat, lam, hdiag, left_ops, right_operators, couple, blockmask)


def solution(mesh):
    placed = (
        P(("seg", "ops"), None),
        P(("seg", "ops")),
        P(("seg", "ops"), None),
        P("seg", "ops", None, None),
        P("seg", "ops", None, None),
        P("seg", "ops", None),
        P("seg", "ops", None),
    )
    return jax.shard_map(
        body,
        mesh=mesh,
        in_specs=placed,
        out_specs=(P(("seg", "ops"), None), P("seg")),
        check_vma=False,
    )
```
